32 devices in a mesh: band: 4 (over z), tile: 8 (over y, x, core).
Axes of the slice: x: 2, y: 2, z: 4, core: 2. Of those that a mesh axis runs over, the one named last changes fastest.
Arguments:
- frames: bfloat16 [256, 512, 1024], P('band', 'tile'), may hold values from -6 to 6
- probe: float32 [2, 128, 128], replicated, may hold values from -6 to 6
- rho_weights: float32 [2, 256], P(None, 'tile'), may hold values from -0.375 to 0.375
- phase_offsets: int32 [4, 8], replicated, may hold values from 0 to 1023
- margin_widths: int32 [4, 8], replicated, may hold values from 8 to 32, as said below
Outputs:
- object_field: float32 [2, 256, 512], P(None, 'band', 'tile')
The draws below stay inside these ranges and needn't reach their ends.
Inputs may be any that keep to these rules, and one draw needn't show every extreme that they name: `margin_widths`: some tile has a margin of exactly 32.
All inputs are finite; a program needn't handle non-finite values.
Results may differ from the reference program's by a relative error of at most 0.012.
Values may be sent and summed in bfloat16 or wider, within the bound.
No kernel may reach another device: no remote copies, remote signals or barrier semaphores. Data moves between devices by JAX's collectives and lax.ppermute only.
A program may use at most 128 MiB of HBM per device.

```python
import math
import jax
import jax.numpy as jnp
from jax import lax

DY = 32
DX = 32
RW = 16
TS = 128
MARGIN = 32
TPB = 8
TI = 64
DET = 1024
RHO = 256
BANDS = 4
NR = 256
NC = 512


def draw_margin_widths(key, part):
    first_key = jax.random.fold_in(key, 11)
    second_key = jax.random.fold_in(key, 12)
    widths = jax.random.randint(first_key, (BANDS * TPB,), MARGIN // 4, MARGIN + 1)
    spot = jax.random.randint(second_key, (), 0, BANDS * TPB)
    widths = jnp.where(jnp.arange(BANDS * TPB) == spot, MARGIN, widths)
    return widths.reshape(BANDS, TPB).astype(jnp.int32)


def touch_ends(values, rng, low, largest):
    spot = [jax.random.randint(jax.random.fold_in(rng, axis), (), 0, length) for axis, length in enumerate(values.shape)]
    longest = values.shape.index(max(values.shape))
    beside = spot[:longest] + [(spot[longest] + 1) % values.shape[longest]] + spot[longest + 1:]
    return values.at[tuple(spot)].set(low).at[tuple(beside)].set(largest)


def block_scale(rng, shape, shards, low, high):
    factor_of, own = 1.0, jax.random.fold_in(rng, 6)
    for axis_at, parts in shards:
        heights = jnp.exp(jax.random.uniform(jax.random.fold_in(own, axis_at), (parts,), jnp.float32, low / len(shards), high / len(shards)))
        factor_of = factor_of * jnp.repeat(heights, shape[axis_at] // parts).reshape([-1 if axis == axis_at else 1 for axis in range(len(shape))])
    return factor_of


def scatter_about(key, shape, deviation, limit, split=(), kind=jnp.bfloat16):
    result = jax.random.normal(key, shape, jnp.float32) * deviation
    if len(split) > 0:
        result = block_scale(key, shape, split, -0.22, 0.18) * result
    return jnp.clip(result, min=-limit, max=limit).astype(kind)


def setup_inputs(seed: int = 0) -> dict:
    seeds = jax.random.split(jax.random.key(seed), 6)
    return {
        "frames": scatter_about(seeds[0], (NR, NC, DET), 1.0, 6.0, ((0, 4), (1, 8))),
        "probe": scatter_about(seeds[1], (2, TS, TS), 1.0, 6.0, (), jnp.float32),
        "rho_weights": scatter_about(seeds[2], (2, RHO), RHO ** -0.5, 0.375, ((1, 8),), jnp.float32),
        "phase_offsets": touch_ends(jax.random.randint(seeds[3], (BANDS, TPB), 0, 1024), jax.random.fold_in(seeds[3], 1), 0, 1023).astype(jnp.int32),
        "margin_widths": draw_margin_widths(jax.random.fold_in(seeds[5], 71), 0),
    }


wiener_floor = 1.0
phase_steps = 1024.0

def detector_table(span, size_y, size_x):
    index_y = jnp.arange(size_y, dtype=jnp.int32)
    index_x = jnp.arange(size_x, dtype=jnp.int32)
    shifts = jnp.arange(span, dtype=jnp.int32) - span // 2
    turns_y = (shifts[:, None] * index_y[None, :] % size_y).astype(jnp.float32) / size_y
    turns_x = (shifts[:, None] * index_x[None, :] % size_x).astype(jnp.float32) / size_x
    theta = 2.0 * math.pi * (turns_y[:, None, :, None] + turns_x[None, :, None, :])
    scale = 1.0 / math.sqrt(size_y * size_x)
    table = jnp.stack([jnp.cos(theta), jnp.sin(theta)], axis=2) * scale
    return table.reshape(span * span * 2, size_y * size_x).astype(jnp.bfloat16)

def scan_table(size, forward):
    index = jnp.arange(size, dtype=jnp.int32)
    theta = 2.0 * math.pi * (index[:, None] * index[None, :] % size).astype(jnp.float32) / size
    cosine = jnp.cos(theta) / math.sqrt(size)
    sine = jnp.sin(theta) / math.sqrt(size)
    if forward:
        rows = [jnp.stack([cosine, sine], 1), jnp.stack([-sine, cosine], 1)]
    else:
        rows = [jnp.stack([cosine, -sine], 1), jnp.stack([sine, cosine], 1)]
    return jnp.stack(rows, 0)

def transform(rows_table, cols_table, field):
    high = lax.Precision.HIGHEST
    first = jnp.einsum('aqpy,rpyx->raqx', rows_table.astype(jnp.float32), field.astype(jnp.float32), precision=high).astype(jnp.bfloat16)
    first = lax.optimization_barrier(first)
    return jnp.einsum('bkpx,rpqx->rbqk', cols_table.astype(jnp.float32), first.astype(jnp.float32), precision=high)

def product_field(doubled, shift_y, shift_x):
    size = doubled.shape[1] // 2
    zero = jnp.zeros((), jnp.int32)
    moved = lax.dynamic_slice(doubled, (zero, shift_y.astype(jnp.int32), shift_x.astype(jnp.int32)), (2, size, size))
    base = doubled[:, :size, :size]
    real = base[0] * moved[0] + base[1] * moved[1]
    imag = base[1] * moved[0] - base[0] * moved[1]
    return jnp.stack([real, imag]).astype(jnp.bfloat16)

def probe_wigner(probe, first_rho, count, span, rows_table, cols_table):
    size = probe.shape[1]
    rho = first_rho + jnp.arange(count, dtype=jnp.int32)
    shift_y = (rho // span - span // 2) % size
    shift_x = (rho % span - span // 2) % size
    doubled = jnp.concatenate([probe, probe], 1)
    doubled = jnp.concatenate([doubled, doubled], 2)
    fields = jax.vmap(lambda sy, sx: product_field(doubled, sy, sx))(shift_y, shift_x)
    return transform(rows_table, cols_table, fields)

def wiener(spectrum, chi):
    denom = chi[:, 0] * chi[:, 0] + chi[:, 1] * chi[:, 1] + wiener_floor
    real = (spectrum[:, 0] * chi[:, 0] + spectrum[:, 1] * chi[:, 1]) / denom
    imag = (spectrum[:, 1] * chi[:, 0] - spectrum[:, 0] * chi[:, 1]) / denom
    return jnp.stack([real, imag], 1)

def weighted_sum(decon, weights):
    high = lax.Precision.HIGHEST
    real = jnp.einsum('r,rqk->qk', weights[0], decon[:, 0], precision=high) - jnp.einsum('r,rqk->qk', weights[1], decon[:, 1], precision=high)
    imag = jnp.einsum('r,rqk->qk', weights[0], decon[:, 1], precision=high) + jnp.einsum('r,rqk->qk', weights[1], decon[:, 0], precision=high)
    return jnp.stack([real, imag])

def inverse(table, spec):
    high = lax.Precision.HIGHEST
    middle = jnp.einsum('aypq,pqk->ayk', table, spec, precision=high)
    return jnp.einsum('bxpk,pyk->byx', table, middle, precision=high)

def window(width, size, margin):
    index = jnp.arange(size, dtype=jnp.int32)
    inside = (index >= margin - width) & (index < size - margin + width)
    line = inside.astype(jnp.float32)
    return line[:, None] * line[None, :]

def place(field, phase, mask):
    angle = phase.astype(jnp.float32) * (2.0 * math.pi / phase_steps)
    real = field[0] * jnp.cos(angle) - field[1] * jnp.sin(angle)
    imag = field[0] * jnp.sin(angle) + field[1] * jnp.cos(angle)
    return jnp.stack([real, imag]) * mask

def coverage(widths, inner, margin, row_start, rows, col_start, cols):
    bands_n, per_band = widths.shape
    flat = jnp.arange(bands_n * per_band, dtype=jnp.int32)
    tile_band = flat // per_band
    tile_col = flat % per_band
    width = widths.reshape(-1)
    row_ids = row_start + jnp.arange(rows, dtype=jnp.int32)
    col_ids = col_start + jnp.arange(cols, dtype=jnp.int32)
    row_in = ((row_ids[None, :] >= (tile_band * inner - width)[:, None]) & (row_ids[None, :] < (tile_band * inner + inner + width)[:, None])).astype(jnp.float32)
    col_in = ((col_ids[None, :] >= (tile_col * inner - width)[:, None]) & (col_ids[None, :] < (tile_col * inner + inner + width)[:, None])).astype(jnp.float32)
    return jnp.dot(row_in.T, col_in, precision=lax.Precision.HIGHEST)

def reference(frames, probe, rho_weights, phase_offsets, margin_widths):
    table = detector_table(RW, DY, DX)

    def band_spectra(block):
        return jnp.dot(table, block.T, preferred_element_type=jnp.float32).astype(jnp.bfloat16)
    spectra = lax.map(band_spectra, frames.reshape(BANDS, TI * NC, DET))
    spectra = spectra.reshape(BANDS, RHO, 2, TI, NC).transpose(1, 2, 0, 3, 4).reshape(RHO, 2, NR, NC)
    padded = jnp.pad(spectra, ((0, 0), (0, 0), (MARGIN, MARGIN), (MARGIN, MARGIN)))
    forward_table = scan_table(TS, True).astype(jnp.bfloat16)
    inverse_table = scan_table(TS, False)
    chi = probe_wigner(probe, jnp.zeros((), jnp.int32), RHO, RW, forward_table, forward_table)
    zero = jnp.zeros((), jnp.int32)

    def add_tile(canvas, tile):
        band_id = tile // TPB
        col_id = tile % TPB
        row_at = (band_id * TI).astype(jnp.int32)
        col_at = (col_id * TI).astype(jnp.int32)
        block = lax.dynamic_slice(padded, (zero, zero, row_at, col_at), (RHO, 2, TS, TS))
        mask = window(margin_widths[band_id, col_id], TS, MARGIN)
        block = block * mask.astype(jnp.bfloat16)
        spectrum = transform(forward_table, forward_table, block)
        decon = wiener(spectrum, chi)
        spec = weighted_sum(decon, rho_weights)
        field = inverse(inverse_table, spec)
        piece = place(field, phase_offsets[band_id, col_id], mask)
        old = lax.dynamic_slice(canvas, (zero, row_at, col_at), (2, TS, TS))
        return (lax.dynamic_update_slice(canvas, old + piece, (zero, row_at, col_at)), None)
    canvas = jnp.zeros((2, NR + 2 * MARGIN, NC + 2 * MARGIN), jnp.float32)
    canvas, unused = lax.scan(add_tile, canvas, jnp.arange(BANDS * TPB, dtype=jnp.int32))
    count = coverage(margin_widths, TI, MARGIN, 0, NR, 0, NC)
    return canvas[:, MARGIN:MARGIN + NR, MARGIN:MARGIN + NC] / count[None]
```

```python
import functools
import math

import jax
import jax.numpy as jnp
import numpy as np
from jax import lax
from jax.experimental import pallas as pl
from jax.experimental.pallas import tpu as pltpu
from jax.sharding import PartitionSpec as P

DY = 32
DX = 32
RW = 16
TS = 128
MARGIN = 32
INNER = TS - 2 * MARGIN
HALF = INNER // 2
GY = 3
GX = 4
phase_steps = 1024.0

MIB = 1024 * 1024


class Plan:
    def __init__(self, cols):
        lo = -(RW // 2)
        paired, alone = [], []
        for ry in range(lo, lo + RW):
            for rx in range(lo, lo + RW):
                if ry == lo or rx == lo or (ry == 0 and rx == 0):
                    alone.append((ry, rx))
                elif ry > 0 or (ry == 0 and rx > 0):
                    paired.append((ry, rx))
        self.cols = cols
        self.group = TS // cols
        self.lists = [paired[c :: self.group] + alone[c :: self.group] for c in range(self.group)]
        self.paired = len(paired) // self.group
        self.share = len(self.lists[0])
        self.chunk = max(c for c in (4, 3, 2, 1) if self.share % c == 0)
        self.steps = self.share // self.chunk

    def shift_tables(self):
        rows = np.zeros((self.group, 4, self.share), np.int32)
        for c in range(self.group):
            for i, (ry, rx) in enumerate(self.lists[c]):
                rows[c, 0, i] = ry
                rows[c, 1, i] = rx
                rows[c, 2, i] = rho_of(ry, rx)
                rows[c, 3, i] = rho_of(-ry, -rx) if i < self.paired else rho_of(ry, rx)
        return rows

    def groups(self, count):
        return [list(range(at, at + self.group)) for at in range(0, count, self.group)]

    def scan_tables(self):
        x = np.arange(self.cols)
        halves = []
        for gx in range(GX):
            rows = [forward_right(c * self.cols + x - (gx - 1) * INNER + MARGIN) for c in range(self.group)]
            halves.append(np.concatenate(rows).reshape(2, TS, 2 * TS))
        return as_bf16(np.stack(halves))


HIGHEST_RY = RW // 2


def rho_of(ry, rx):
    return (ry + RW // 2) * RW + rx + RW // 2


def detector_table(order):
    ky = np.arange(DY)
    kx = np.arange(DX)
    out = np.zeros((2, len(order), DY * DX), np.float64)
    for i, (ry, rx) in enumerate(order):
        turns = ((ry * ky) % DY)[:, None] / DY + ((rx * kx) % DX)[None, :] / DX
        theta = 2.0 * math.pi * turns.reshape(-1)
        out[0, i] = np.cos(theta)
        out[1, i] = np.sin(theta)
    return as_bf16(out.reshape(2 * len(order), DY * DX) / math.sqrt(DY * DX))


def waves():
    index = np.arange(TS)
    theta = 2.0 * math.pi * (index[:, None] * index[None, :] % TS) / TS
    return np.cos(theta) / math.sqrt(TS), np.sin(theta) / math.sqrt(TS)


def forward_right(positions):
    cosine, sine = waves()
    valid = ((positions >= 0) & (positions < TS)).astype(np.float64)[:, None]
    at = np.clip(positions, 0, TS - 1)
    c, s = cosine[at] * valid, sine[at] * valid
    return np.block([[c, -s], [s, c]])


def forward_left(positions):
    return forward_right(positions).T


def inverse_tables():
    cosine, sine = waves()
    right = np.block([[cosine, sine], [-sine, cosine]]).astype(np.float32)
    real = np.concatenate([cosine, -sine], 1).astype(np.float32)
    imag = np.concatenate([sine, cosine], 1).astype(np.float32)
    return right, np.concatenate([real, imag], 0)


def as_bf16(table):
    return table.astype(np.float32).astype(jnp.bfloat16)


def iota(shape, dim):
    return lax.broadcasted_iota(jnp.int32, shape, dim)


ROWS_AT_ONCE = 16


def detector_kernel(table_ref, frames_ref, own_ref, other_ref, buf):
    share = own_ref.shape[0]
    both = 2 * share
    table = table_ref[0]
    lane = iota((both, TS), 1)
    low = lane < INNER
    for part in range(2):
        rows = ROWS_AT_ONCE // 2
        block = frames_ref[part * rows : (part + 1) * rows].reshape(rows * INNER, DY * DX)
        out = lax.dot_general(table, block, (((1,), (1,)), ((), ())), preferred_element_type=jnp.float32)
        for pair in range(rows // 2):
            c = out[:both, pair * TS : (pair + 1) * TS]
            s = out[both:, pair * TS : (pair + 1) * TS]
            first = jnp.where(low, c, pltpu.roll(s, INNER, 1))
            second = jnp.where(low, pltpu.roll(c, INNER, 1), s)
            y = part * rows + pair * 2
            buf[pl.ds(y, both, stride=ROWS_AT_ONCE), :] = first
            buf[pl.ds(y + 1, both, stride=ROWS_AT_ONCE), :] = second
    own_ref[...] = buf[: share * ROWS_AT_ONCE].reshape(share, ROWS_AT_ONCE, TS).astype(jnp.bfloat16)
    other_ref[...] = buf[share * ROWS_AT_ONCE :].reshape(share, ROWS_AT_ONCE, TS).astype(jnp.bfloat16)


def detector(plan, place, frames):
    share = plan.share
    tables = jnp.asarray(np.stack([detector_table(plan.lists[c] + plan.lists[1 - c]) for c in range(2)]))
    shape = jax.ShapeDtypeStruct((share, INNER, TS), jnp.bfloat16)
    spec = pl.BlockSpec((share, ROWS_AT_ONCE, TS), lambda i, place: (0, i, 0))

    def body(place_ref, *refs):
        detector_kernel(*refs)

    return pl.pallas_call(
        body,
        out_shape=(shape, shape),
        grid_spec=pltpu.PrefetchScalarGridSpec(
            num_scalar_prefetch=1,
            grid=(INNER // ROWS_AT_ONCE,),
            in_specs=[
                pl.BlockSpec((1, 4 * share, DY * DX), lambda i, place: (place[2], 0, 0)),
                pl.BlockSpec((ROWS_AT_ONCE, INNER, DY * DX), lambda i, place: (i, 0, 0)),
            ],
            out_specs=[spec, spec],
            scratch_shapes=[pltpu.VMEM((2 * share * ROWS_AT_ONCE, TS), jnp.float32)],
        ),
        compiler_params=pltpu.CompilerParams(vmem_limit_bytes=40 * MIB),
        name="detector",
    )(place, tables, frames)


def detector_any(plan, frames):
    rows, cols, pixels = frames.shape
    table = detector_table([rho for part in plan.lists for rho in part])
    spectra = lax.dot_general(
        jnp.asarray(table),
        frames.reshape(rows * cols, pixels),
        (((1,), (1,)), ((), ())),
        preferred_element_type=jnp.float32,
    ).astype(jnp.bfloat16)
    spectra = spectra.reshape(2, plan.group, plan.share, rows, cols)
    return jnp.transpose(spectra, (1, 2, 3, 0, 4)).reshape(plan.group, plan.share, rows, 2 * cols)


def shared_spectra(plan, place, frames):
    count = lax.axis_size("tile")
    if plan.group == 2:
        own, other = detector(plan, place, frames)
        return own, lax.ppermute(other, "tile", [(i, i ^ 1) for i in range(count)])
    spectra = detector_any(plan, frames)
    taken = lax.all_to_all(
        spectra, "tile", split_axis=0, concat_axis=0, axis_index_groups=plan.groups(count), tiled=True
    )
    taken = jnp.transpose(taken.reshape(2, plan.group // 2, plan.share, INNER, 2 * plan.cols), (0, 2, 3, 1, 4))
    taken = taken.reshape(2, plan.share, INNER, TS)
    return taken[0], taken[1]


ROW_BLOCK = 8


def filter_kernel(plan, place_ref, shift_ref, weight_ref, probe_ref, right_ref, left_ref, wave_ref, row_ref, out_ref,
                  ey, first_buf, stack_buf, chi_buf):
    core = place_ref[2]
    step = pl.program_id(0)
    chunk = plan.chunk

    @pl.when(step == 0)
    def _():
        ey[0, 0] = jnp.ones((TS, TS), jnp.float32)
        ey[0, 1] = jnp.zeros((TS, TS), jnp.float32)
        for n in range(1, HIGHEST_RY):
            r, i = ey[n - 1, 0], ey[n - 1, 1]
            a, b = wave_ref[0], wave_ref[1]
            ey[n, 0] = r * a - i * b
            ey[n, 1] = r * b + i * a

    base_r, base_i = probe_ref[0], probe_ref[1]
    for r in range(chunk):
        at = step * chunk + r
        sy = shift_ref[core, 0, at]
        sx = shift_ref[core, 1, at]
        back_y = lax.rem(TS - sy, TS)
        back_x = lax.rem(TS - sx, TS)
        moved_r = pltpu.roll(pltpu.roll(base_r, back_y, 0), back_x, 1)
        moved_i = pltpu.roll(pltpu.roll(base_i, back_y, 0), back_x, 1)
        real = base_r * moved_r + base_i * moved_i
        imag = base_i * moved_r - base_r * moved_i
        first_buf[r * TS : (r + 1) * TS, :TS] = real.astype(jnp.bfloat16)
        first_buf[r * TS : (r + 1) * TS, TS:] = imag.astype(jnp.bfloat16)
    middle = jnp.dot(first_buf[...], right_ref[...], preferred_element_type=jnp.float32).astype(jnp.bfloat16)
    for r in range(chunk):
        for p in range(2):
            stack_buf[p * TS : (p + 1) * TS, r * TS : (r + 1) * TS] = middle[r * TS : (r + 1) * TS, p * TS : (p + 1) * TS]
    chi_buf[...] = jnp.dot(left_ref[...], stack_buf[...], preferred_element_type=jnp.float32)
    for r in range(chunk):
        at = step * chunk + r
        sy = shift_ref[core, 0, at]
        sx = shift_ref[core, 1, at]
        wr = weight_ref[0, shift_ref[core, 2, at]]
        wi = weight_ref[1, shift_ref[core, 2, at]]
        keep = (at < plan.paired).astype(jnp.float32)
        vr = weight_ref[0, shift_ref[core, 3, at]] * keep
        vi = -weight_ref[1, shift_ref[core, 3, at]] * keep
        n = jnp.clip(sy, 0, HIGHEST_RY - 1)
        ex_r = row_ref[0, pl.ds(sx + RW // 2, 1), :]
        ex_i = row_ref[1, pl.ds(sx + RW // 2, 1), :]
        er = jnp.broadcast_to(vr * ex_r - vi * ex_i, (ROW_BLOCK, TS))
        ei = jnp.broadcast_to(vr * ex_i + vi * ex_r, (ROW_BLOCK, TS))
        for v in range(TS // ROW_BLOCK):
            rows = slice(v * ROW_BLOCK, (v + 1) * ROW_BLOCK)
            cr = chi_buf[v * ROW_BLOCK : (v + 1) * ROW_BLOCK, r * TS : (r + 1) * TS]
            ci = chi_buf[TS + v * ROW_BLOCK : TS + (v + 1) * ROW_BLOCK, r * TS : (r + 1) * TS]
            inv = 1.0 / (cr * cr + ci * ci + 1.0)
            hr = cr * inv
            hi = -ci * inv
            out_ref[r, 0, rows] = wr * hr - wi * hi
            out_ref[r, 1, rows] = wr * hi + wi * hr
            yr = ey[n, 0, rows]
            yi = ey[n, 1, rows]
            pr = yr * er - yi * ei
            pi = yr * ei + yi * er
            out_ref[r, 2, rows] = pr * hr - pi * hi
            out_ref[r, 3, rows] = pr * hi + pi * hr


def filters(plan, place, weights, probe):
    chunk = plan.chunk
    index = np.arange(TS)
    wave = np.stack([np.cos(2 * math.pi * index / TS), np.sin(2 * math.pi * index / TS)])
    wave = np.broadcast_to(wave[:, :, None], (2, TS, TS)).astype(np.float32)
    shifts = np.arange(RW) - RW // 2
    theta = 2.0 * math.pi * (shifts[:, None] * index[None, :] % TS) / TS
    row = np.stack([np.cos(theta), np.sin(theta)]).astype(np.float32)
    right = forward_right(index)
    smem = pl.BlockSpec(memory_space=pltpu.SMEM)
    full = lambda *shape: pl.BlockSpec(shape, lambda i: (0,) * len(shape))
    return pl.pallas_call(
        functools.partial(filter_kernel, plan),
        out_shape=jax.ShapeDtypeStruct((plan.share, 4, TS, TS), jnp.float32),
        grid=(plan.steps,),
        in_specs=[
            smem,
            smem,
            smem,
            full(2, TS, TS),
            full(2 * TS, 2 * TS),
            full(2 * TS, 2 * TS),
            full(2, TS, TS),
            full(2, RW, TS),
        ],
        out_specs=pl.BlockSpec((chunk, 4, TS, TS), lambda i: (i, 0, 0, 0)),
        scratch_shapes=[
            pltpu.VMEM((HIGHEST_RY, 2, TS, TS), jnp.float32),
            pltpu.VMEM((chunk * TS, 2 * TS), jnp.bfloat16),
            pltpu.VMEM((2 * TS, chunk * TS), jnp.bfloat16),
            pltpu.VMEM((2 * TS, chunk * TS), jnp.float32),
        ],
        compiler_params=pltpu.CompilerParams(vmem_limit_bytes=40 * MIB),
        name="filters",
    )(
        place,
        jnp.asarray(plan.shift_tables()),
        weights,
        probe,
        jnp.asarray(as_bf16(right)),
        jnp.asarray(as_bf16(right.T)),
        jnp.asarray(wave),
        jnp.asarray(row),
    )


def in_window(index, width):
    return (index >= MARGIN - width) & (index < TS - MARGIN + width)


def decon_kernel(plan, place_ref, width_ref, phasor_ref, own_ref, got_ref, filt_ref, cols_ref, mid_ref, edge_ref,
                 inv_right_ref, inv_left_ref, left_out, mid_out, right_out,
                 cols_buf, edge_buf, acc, z_mid, z_edge, s_buf):
    step = pl.program_id(0)
    band = place_ref[0]
    chip = place_ref[1]
    side_first = place_ref[3]
    chunk = plan.chunk

    @pl.when(step == 0)
    def _():
        row = iota((TS, 2 * TS), 0)
        x = row // (2 * plan.cols) * plan.cols + row % plan.cols
        lane = iota((2 * TS, 2 * HALF), 1)
        y = jnp.where(lane < HALF, lane, lane - HALF)
        for gx in range(GX):
            for o in range(2):
                side = side_first if o == 0 else 1 - side_first
                table = cols_ref[gx, pl.ds(side, 1)][0].astype(jnp.float32)
                xt = side * INNER + x - (gx - 1) * INNER + MARGIN
                for gy in range(GY):
                    width = width_ref[band + gy, 2 * chip + gx]
                    kept = jnp.where(in_window(xt, width), table, 0.0)
                    cols_buf[gy, gx, o * TS : (o + 1) * TS] = kept.astype(jnp.bfloat16)
            for e in range(2):
                width = width_ref[band + 2 * e, 2 * chip + gx]
                yt = y + (TS - HALF if e == 0 else 0)
                kept = jnp.where(in_window(yt, width), edge_ref[e].astype(jnp.float32), 0.0)
                edge_buf[e, gx] = kept.astype(jnp.bfloat16)
        acc[...] = jnp.zeros(acc.shape, jnp.float32)

    def put(buf, at, z, rows):
        z = z.astype(jnp.bfloat16)
        for r in range(chunk):
            for p in range(2):
                buf[at + (slice(p * rows, (p + 1) * rows), slice(r * TS, (r + 1) * TS))] = z[
                    r * rows : (r + 1) * rows, p * TS : (p + 1) * TS
                ]

    def data(first, last):
        rows = last - first
        own = own_ref[:, first:last, :].reshape(chunk * rows, TS)
        got = got_ref[:, first:last, :].reshape(chunk * rows, TS)
        return jnp.concatenate([own, got], 1)

    pieces = [data(0, HALF), data(0, INNER), data(HALF, INNER)]
    for gx in range(GX):
        for gy in range(GY):
            z = jnp.dot(pieces[gy], cols_buf[gy, gx], preferred_element_type=jnp.float32)
            if gy == 1:
                put(z_mid, (gx,), z, INNER)
            else:
                put(z_edge, (gy // 2, gx), z, HALF)

    def products(gx):
        s_buf[gx, 0] = jnp.dot(edge_buf[0, gx], z_edge[0, gx], preferred_element_type=jnp.float32)
        s_buf[gx, 1] = jnp.dot(mid_ref[...], z_mid[gx], preferred_element_type=jnp.float32)
        s_buf[gx, 2] = jnp.dot(edge_buf[1, gx], z_edge[1, gx], preferred_element_type=jnp.float32)

    def gather(gx):
        for v in range(TS // ROW_BLOCK):
            rows = slice(v * ROW_BLOCK, (v + 1) * ROW_BLOCK)
            low = slice(TS + v * ROW_BLOCK, TS + (v + 1) * ROW_BLOCK)
            sums = [[acc[gy, gx, c, rows] for c in range(4)] for gy in range(GY)]
            for r in range(chunk):
                lanes = slice(r * TS, (r + 1) * TS)
                ar, ai, br, bi = [filt_ref[r, c, rows] for c in range(4)]
                for gy in range(GY):
                    sr = s_buf[gx, gy, rows, lanes]
                    si = s_buf[gx, gy, low, lanes]
                    t = sums[gy]
                    sums[gy] = [
                        t[0] + (ar * sr - ai * si),
                        t[1] + (ar * si + ai * sr),
                        t[2] + (br * sr - bi * si),
                        t[3] + (br * si + bi * sr),
                    ]
            for gy in range(GY):
                for c in range(4):
                    acc[gy, gx, c, rows] = sums[gy][c]

    products(0)
    for gx in range(GX):
        if gx + 1 < GX:
            products(gx + 1)
        gather(gx)

    @pl.when(step == plan.steps - 1)
    def _():
        high = lax.Precision.HIGHEST
        for ref in (left_out, mid_out, right_out):
            ref[...] = jnp.zeros(ref.shape, jnp.float32)
        row = iota((TS, TS), 0)
        lane = iota((TS, TS), 1)
        inv_right = inv_right_ref[...]
        for gy in range(GY):
            for gx in range(GX):
                ar, ai, br, bi = [acc[gy, gx, c] for c in range(4)]
                both = jnp.concatenate(
                    [jnp.concatenate([ar + br, ai + bi], 1), jnp.concatenate([ar - br, ai - bi], 1)], 0
                )
                half = jnp.dot(both, inv_right, precision=high, preferred_element_type=jnp.float32)
                plus = jnp.concatenate([half[:TS, :TS], half[:TS, TS:]], 0)
                minus = jnp.concatenate([half[TS:, :TS], half[TS:, TS:]], 0)
                fr = jnp.dot(inv_left_ref[:TS], plus, precision=high, preferred_element_type=jnp.float32)
                fi = jnp.dot(inv_left_ref[TS:], minus, precision=high, preferred_element_type=jnp.float32)
                width = width_ref[band + gy, 2 * chip + gx]
                pc = phasor_ref[0, band + gy, 2 * chip + gx]
                ps = phasor_ref[1, band + gy, 2 * chip + gx]
                inside = in_window(row, width) & in_window(lane, width)
                placed = (jnp.where(inside, fr * pc - fi * ps, 0.0), jnp.where(inside, fr * ps + fi * pc, 0.0))
                start = MARGIN + gx * INNER
                shift = start % TS
                outs = (left_out, mid_out, right_out)
                rows = slice(gy * INNER, gy * INNER + TS)
                for part in range(2):
                    turned = pltpu.roll(placed[part], shift, 1)
                    outs[start // TS][part, rows] += jnp.where(lane >= shift, turned, 0.0)
                    outs[start // TS + 1][part, rows] += jnp.where(lane >= shift, 0.0, turned)


def deconvolve(plan, place, widths, phasors, own, got, filt):
    chunk = plan.chunk
    y = np.arange(INNER)
    mid = as_bf16(forward_left(y + MARGIN))
    edge = np.stack([as_bf16(forward_left(y[:HALF] + TS - HALF)), as_bf16(forward_left(y[:HALF]))])
    inv_right, inv_left = inverse_tables()
    smem = pl.BlockSpec(memory_space=pltpu.SMEM)
    full = lambda *shape: pl.BlockSpec(shape, lambda i: (0,) * len(shape))
    rows = (GY + 1) * INNER
    canvas = jax.ShapeDtypeStruct((2, rows, TS), jnp.float32)
    return pl.pallas_call(
        functools.partial(decon_kernel, plan),
        out_shape=(canvas,) * 3,
        grid=(plan.steps,),
        in_specs=[
            smem,
            smem,
            smem,
            pl.BlockSpec((chunk, INNER, TS), lambda i: (i, 0, 0)),
            pl.BlockSpec((chunk, INNER, TS), lambda i: (i, 0, 0)),
            pl.BlockSpec((chunk, 4, TS, TS), lambda i: (i, 0, 0, 0)),
            full(GX, 2, TS, 2 * TS),
            full(2 * TS, 2 * INNER),
            full(2, 2 * TS, 2 * HALF),
            full(2 * TS, 2 * TS),
            full(2 * TS, 2 * TS),
        ],
        out_specs=(full(2, rows, TS),) * 3,
        scratch_shapes=[
            pltpu.VMEM((GY, GX, 2 * TS, 2 * TS), jnp.bfloat16),
            pltpu.VMEM((2, GX, 2 * TS, 2 * HALF), jnp.bfloat16),
            pltpu.VMEM((GY, GX, 4, TS, TS), jnp.float32),
            pltpu.VMEM((GX, 2 * INNER, chunk * TS), jnp.bfloat16),
            pltpu.VMEM((2, GX, 2 * HALF, chunk * TS), jnp.bfloat16),
            pltpu.VMEM((GX, GY, 2 * TS, chunk * TS), jnp.float32),
        ],
        compiler_params=pltpu.CompilerParams(vmem_limit_bytes=56 * MIB),
        name="deconvolve",
    )(
        place,
        widths,
        phasors,
        own,
        got,
        filt,
        jnp.asarray(plan.scan_tables()),
        jnp.asarray(mid),
        jnp.asarray(edge),
        jnp.asarray(inv_right),
        jnp.asarray(inv_left),
    )


def passed_along(value, axis, steps):
    count = lax.axis_size(axis)
    leading, last = (max(0, -steps), min(count, count - steps))
    if leading >= last:
        return jnp.zeros_like(value)
    return lax.ppermute(value, axis, [(source, source + steps) for source in range(leading, last)])


def own_part(plan, value, member):
    count = lax.axis_size("tile")
    if plan.group != 2:
        return lax.psum_scatter(
            value, "tile", scatter_dimension=2, axis_index_groups=plan.groups(count), tiled=True
        )
    zero = jnp.zeros((), jnp.int32)
    size = value.shape[:2] + (plan.cols,)
    kept = lax.dynamic_slice(value, (zero, zero, member * plan.cols), size)
    sent = lax.dynamic_slice(value, (zero, zero, (1 - member) * plan.cols), size)
    return kept + lax.ppermute(sent, "tile", [(i, i ^ 1) for i in range(count)])


def coverage(widths, inner, row_start, rows, col_start, cols):
    bands_n, per_band = widths.shape
    flat = jnp.arange(bands_n * per_band, dtype=jnp.int32)
    tile_band = flat // per_band
    tile_col = flat % per_band
    width = widths.reshape(-1)
    row_ids = row_start + jnp.arange(rows, dtype=jnp.int32)
    col_ids = col_start + jnp.arange(cols, dtype=jnp.int32)
    row_in = (
        (row_ids[None, :] >= (tile_band * inner - width)[:, None])
        & (row_ids[None, :] < (tile_band * inner + inner + width)[:, None])
    ).astype(jnp.float32)
    col_in = (
        (col_ids[None, :] >= (tile_col * inner - width)[:, None])
        & (col_ids[None, :] < (tile_col * inner + inner + width)[:, None])
    ).astype(jnp.float32)
    return jnp.dot(row_in.T, col_in, precision=lax.Precision.HIGHEST)


def local(frames, probe, rho_weights, phase_offsets, margin_widths):
    band = lax.axis_index("band").astype(jnp.int32)
    column = lax.axis_index("tile").astype(jnp.int32)
    plan = Plan(frames.shape[1])
    member = column % plan.group
    side = member if plan.group == 2 else jnp.zeros((), jnp.int32)
    place = jnp.stack([band, column // plan.group, member, side])
    weights = lax.all_gather(rho_weights, "tile", axis=1, tiled=True)
    widths = jnp.pad(margin_widths, 1)
    angle = phase_offsets.astype(jnp.float32) * (2.0 * math.pi / phase_steps)
    phasors = jnp.pad(jnp.stack([jnp.cos(angle), jnp.sin(angle)]), ((0, 0), (1, 1), (1, 1)))
    own, got = shared_spectra(plan, place, frames)
    filt = filters(plan, place, weights, probe)
    left, mid, right = deconvolve(plan, place, widths, phasors, own, got, filt)
    mid = mid + passed_along(left, "tile", -plan.group) + passed_along(right, "tile", plan.group)
    first = MARGIN + INNER
    mine = (
        mid[:, first : first + INNER]
        + passed_along(mid[:, first + INNER : first + 2 * INNER], "band", 1)
        + passed_along(mid[:, MARGIN:first], "band", -1)
    )
    far_down = passed_along(mid[:, first + 2 * INNER :], "band", 2)
    far_up = passed_along(mid[:, :MARGIN], "band", -2)
    mine = mine + jnp.concatenate([far_down, far_up], 1)
    total = own_part(plan, mine, member)
    count = coverage(margin_widths, INNER, band * INNER, INNER, column * plan.cols, plan.cols)
    return total / count[None]


def solution(mesh):
    return jax.shard_map(
        local,
        mesh=mesh,
        in_specs=(P("band", "tile", None), P(), P(None, "tile"), P(), P()),
        out_specs=P(None, "band", "tile"),
        check_vma=False,
    )
```

```python
import functools
import math

import jax
import jax.numpy as jnp
import numpy as np
from jax import lax
from jax.experimental import pallas as pl
from jax.experimental.pallas import tpu as pltpu
from jax.sharding import PartitionSpec as P

DY = 32
DX = 32
RW = 16
TS = 128
MARGIN = 32
INNER = TS - 2 * MARGIN
HALF = INNER // 2
GY = 3
GX = 4
phase_steps = 1024.0

MIB = 1024 * 1024


class Plan:
    def __init__(self, cols):
        lo = -(RW // 2)
        paired, alone = [], []
        for ry in range(lo, lo + RW):
            for rx in range(lo, lo + RW):
                if ry == lo or rx == lo or (ry == 0 and rx == 0):
                    alone.append((ry, rx))
                elif ry > 0 or (ry == 0 and rx > 0):
                    paired.append((ry, rx))
        self.cols = cols
        self.group = TS // cols
        self.lists = [paired[c :: self.group] + alone[c :: self.group] for c in range(self.group)]
        self.paired = len(paired) // self.group
        self.share = len(self.lists[0])
        self.chunk = 4 if self.share % 4 == 0 else 2
        self.steps = self.share // self.chunk
        self.paired_steps = -(-self.paired // self.chunk)

    def shift_tables(self):
        rows = np.zeros((self.group, 4, self.share), np.int32)
        for c in range(self.group):
            for i, (ry, rx) in enumerate(self.lists[c]):
                rows[c, 0, i] = ry
                rows[c, 1, i] = rx
                rows[c, 2, i] = rho_of(ry, rx)
                rows[c, 3, i] = rho_of(-ry, -rx) if i < self.paired else rho_of(ry, rx)
        return rows

    def groups(self, count):
        return [list(range(at, at + self.group)) for at in range(0, count, self.group)]

    def scan_tables(self):
        x = np.arange(self.cols)
        halves = []
        for gx in range(GX):
            rows = [forward_right(c * self.cols + x - (gx - 1) * INNER + MARGIN) for c in range(self.group)]
            halves.append(np.concatenate(rows).reshape(2, TS, 2 * TS))
        return as_bf16(np.stack(halves))


HIGHEST_RY = RW // 2


def rho_of(ry, rx):
    return (ry + RW // 2) * RW + rx + RW // 2


def detector_table(order):
    ky = np.arange(DY)
    kx = np.arange(DX)
    out = np.zeros((2, len(order), DY * DX), np.float64)
    for i, (ry, rx) in enumerate(order):
        turns = ((ry * ky) % DY)[:, None] / DY + ((rx * kx) % DX)[None, :] / DX
        theta = 2.0 * math.pi * turns.reshape(-1)
        out[0, i] = np.cos(theta)
        out[1, i] = np.sin(theta)
    return as_bf16(out.reshape(2 * len(order), DY * DX) / math.sqrt(DY * DX))


def waves():
    index = np.arange(TS)
    theta = 2.0 * math.pi * (index[:, None] * index[None, :] % TS) / TS
    return np.cos(theta) / math.sqrt(TS), np.sin(theta) / math.sqrt(TS)


def forward_right(positions):
    cosine, sine = waves()
    valid = ((positions >= 0) & (positions < TS)).astype(np.float64)[:, None]
    at = np.clip(positions, 0, TS - 1)
    c, s = cosine[at] * valid, sine[at] * valid
    return np.block([[c, -s], [s, c]])


def forward_left(positions):
    return forward_right(positions).T


def inverse_tables():
    cosine, sine = waves()
    right = np.block([[cosine, sine], [-sine, cosine]]).astype(np.float32)
    real = np.concatenate([cosine, -sine], 1).astype(np.float32)
    imag = np.concatenate([sine, cosine], 1).astype(np.float32)
    return right, np.concatenate([real, imag], 0)


def as_bf16(table):
    return table.astype(np.float32).astype(jnp.bfloat16)


def iota(shape, dim):
    return lax.broadcasted_iota(jnp.int32, shape, dim)


ROWS_AT_ONCE = 16


def detector_kernel(table_ref, frames_ref, own_ref, other_ref, buf):
    share = own_ref.shape[0]
    both = 2 * share
    table = table_ref[0]
    lane = iota((both, TS), 1)
    low = lane < INNER
    for part in range(2):
        rows = ROWS_AT_ONCE // 2
        block = frames_ref[part * rows : (part + 1) * rows].reshape(rows * INNER, DY * DX)
        out = lax.dot_general(table, block, (((1,), (1,)), ((), ())), preferred_element_type=jnp.float32)
        for pair in range(rows // 2):
            c = out[:both, pair * TS : (pair + 1) * TS]
            s = out[both:, pair * TS : (pair + 1) * TS]
            first = jnp.where(low, c, pltpu.roll(s, INNER, 1))
            second = jnp.where(low, pltpu.roll(c, INNER, 1), s)
            y = part * rows + pair * 2
            buf[pl.ds(y, both, stride=ROWS_AT_ONCE), :] = first
            buf[pl.ds(y + 1, both, stride=ROWS_AT_ONCE), :] = second
    own_ref[...] = buf[: share * ROWS_AT_ONCE].reshape(share, ROWS_AT_ONCE, TS).astype(jnp.bfloat16)
    other_ref[...] = buf[share * ROWS_AT_ONCE :].reshape(share, ROWS_AT_ONCE, TS).astype(jnp.bfloat16)


def detector(plan, place, frames):
    share = plan.share
    tables = jnp.asarray(np.stack([detector_table(plan.lists[c] + plan.lists[1 - c]) for c in range(2)]))
    shape = jax.ShapeDtypeStruct((share, INNER, TS), jnp.bfloat16)
    spec = pl.BlockSpec((share, ROWS_AT_ONCE, TS), lambda i, place: (0, i, 0))

    def body(place_ref, *refs):
        detector_kernel(*refs)

    return pl.pallas_call(
        body,
        out_shape=(shape, shape),
        grid_spec=pltpu.PrefetchScalarGridSpec(
            num_scalar_prefetch=1,
            grid=(INNER // ROWS_AT_ONCE,),
            in_specs=[
                pl.BlockSpec((1, 4 * share, DY * DX), lambda i, place: (place[2], 0, 0)),
                pl.BlockSpec((ROWS_AT_ONCE, INNER, DY * DX), lambda i, place: (i, 0, 0)),
            ],
            out_specs=[spec, spec],
            scratch_shapes=[pltpu.VMEM((2 * share * ROWS_AT_ONCE, TS), jnp.float32)],
        ),
        compiler_params=pltpu.CompilerParams(vmem_limit_bytes=40 * MIB),
        name="detector",
    )(place, tables, frames)


def detector_any(plan, frames):
    rows, cols, pixels = frames.shape
    table = detector_table([rho for part in plan.lists for rho in part])
    spectra = lax.dot_general(
        jnp.asarray(table),
        frames.reshape(rows * cols, pixels),
        (((1,), (1,)), ((), ())),
        preferred_element_type=jnp.float32,
    ).astype(jnp.bfloat16)
    spectra = spectra.reshape(2, plan.group, plan.share, rows, cols)
    return jnp.transpose(spectra, (1, 2, 3, 0, 4)).reshape(plan.group, plan.share, rows, 2 * cols)


def shared_spectra(plan, place, frames):
    count = lax.axis_size("tile")
    if plan.group == 2:
        own, other = detector(plan, place, frames)
        return own, lax.ppermute(other, "tile", [(i, i ^ 1) for i in range(count)])
    spectra = detector_any(plan, frames)
    taken = lax.all_to_all(
        spectra, "tile", split_axis=0, concat_axis=0, axis_index_groups=plan.groups(count), tiled=True
    )
    taken = jnp.transpose(taken.reshape(2, plan.group // 2, plan.share, INNER, 2 * plan.cols), (0, 2, 3, 1, 4))
    taken = taken.reshape(2, plan.share, INNER, TS)
    return taken[0], taken[1]


ROW_BLOCK = 8


def filter_kernel(plan, place_ref, shift_ref, probe_ref, right_ref, left_ref, out_ref, first_buf, stack_buf, chi_buf):
    member = place_ref[2]
    step = pl.program_id(0)
    chunk = plan.chunk
    base_r, base_i = probe_ref[0], probe_ref[1]
    for r in range(chunk):
        at = step * chunk + r
        back_y = lax.rem(TS - shift_ref[member, 0, at], TS)
        back_x = lax.rem(TS - shift_ref[member, 1, at], TS)
        moved_r = pltpu.roll(pltpu.roll(base_r, back_y, 0), back_x, 1)
        moved_i = pltpu.roll(pltpu.roll(base_i, back_y, 0), back_x, 1)
        real = base_r * moved_r + base_i * moved_i
        imag = base_i * moved_r - base_r * moved_i
        first_buf[r * TS : (r + 1) * TS, :TS] = real.astype(jnp.bfloat16)
        first_buf[r * TS : (r + 1) * TS, TS:] = imag.astype(jnp.bfloat16)
    middle = jnp.dot(first_buf[...], right_ref[...], preferred_element_type=jnp.float32).astype(jnp.bfloat16)
    for r in range(chunk):
        for p in range(2):
            stack_buf[p * TS : (p + 1) * TS, r * TS : (r + 1) * TS] = middle[r * TS : (r + 1) * TS, p * TS : (p + 1) * TS]
    chi_buf[...] = jnp.dot(left_ref[...], stack_buf[...], preferred_element_type=jnp.float32)
    for r in range(chunk):
        lanes = slice(r * TS, (r + 1) * TS)
        cr = chi_buf[:TS, lanes]
        ci = chi_buf[TS:, lanes]
        inv = 1.0 / (cr * cr + ci * ci + 1.0)
        out_ref[r, 0] = (cr * inv).astype(jnp.bfloat16)
        out_ref[r, 1] = (-ci * inv).astype(jnp.bfloat16)


def smem():
    return pl.BlockSpec(memory_space=pltpu.SMEM)


def full(*shape):
    return pl.BlockSpec(shape, lambda i: (0,) * len(shape))


def filters(plan, place, probe):
    chunk = plan.chunk
    right = forward_right(np.arange(TS))
    return pl.pallas_call(
        functools.partial(filter_kernel, plan),
        out_shape=jax.ShapeDtypeStruct((plan.share, 2, TS, TS), jnp.bfloat16),
        grid=(plan.steps,),
        in_specs=[smem(), smem(), full(2, TS, TS), full(2 * TS, 2 * TS), full(2 * TS, 2 * TS)],
        out_specs=pl.BlockSpec((chunk, 2, TS, TS), lambda i: (i, 0, 0, 0)),
        scratch_shapes=[
            pltpu.VMEM((chunk * TS, 2 * TS), jnp.bfloat16),
            pltpu.VMEM((2 * TS, chunk * TS), jnp.bfloat16),
            pltpu.VMEM((2 * TS, chunk * TS), jnp.float32),
        ],
        compiler_params=pltpu.CompilerParams(vmem_limit_bytes=40 * MIB),
        name="filters",
    )(place, jnp.asarray(plan.shift_tables()), probe, jnp.asarray(as_bf16(right)), jnp.asarray(as_bf16(right.T)))


def in_window(index, width):
    return (index >= MARGIN - width) & (index < TS - MARGIN + width)


def split(value, axis):
    high = value.astype(jnp.bfloat16)
    low = (value - high.astype(jnp.float32)).astype(jnp.bfloat16)
    return jnp.concatenate([high, low, high], axis)


def table_terms(table, axis):
    high = as_bf16(table)
    low = as_bf16(table - high.astype(np.float64))
    return np.concatenate([high, high, low], axis)


def interleave(items, parts):
    done = 0
    for i, part in enumerate(parts):
        while done < len(items) and done * len(parts) <= i * len(items):
            items[done]()
            done += 1
        part()
    for item in items[done:]:
        item()


def decon_kernel(plan, place_ref, width_ref, phasor_ref, shift_ref, weight_ref, own_ref, got_ref, filt_ref,
                 cols_ref, mid_ref, edge_ref, wave_ref, row_ref, inv_right_ref, inv_left_ref,
                 left_out, mid_out, right_out,
                 cols_buf, edge_buf, acc, z_mid, z_edge, s_buf, ey, gains, canvas):
    step = pl.program_id(0)
    band = place_ref[0]
    chip = place_ref[1]
    member = place_ref[2]
    side_first = place_ref[3]
    chunk = plan.chunk
    f32 = jnp.float32

    def prepare():
        row = iota((TS, 2 * TS), 0)
        x = row // (2 * plan.cols) * plan.cols + row % plan.cols
        lane = iota((2 * TS, 2 * HALF), 1)
        y = jnp.where(lane < HALF, lane, lane - HALF)
        for gx in range(GX):
            for o in range(2):
                side = side_first if o == 0 else 1 - side_first
                table = cols_ref[gx, pl.ds(side, 1)][0].astype(f32)
                xt = side * INNER + x - (gx - 1) * INNER + MARGIN
                for gy in range(GY):
                    width = width_ref[band + gy, 2 * chip + gx]
                    kept = jnp.where(in_window(xt, width), table, 0.0)
                    cols_buf[gy, gx, o * TS : (o + 1) * TS] = kept.astype(jnp.bfloat16)
            for e in range(2):
                width = width_ref[band + 2 * e, 2 * chip + gx]
                yt = y + (TS - HALF if e == 0 else 0)
                kept = jnp.where(in_window(yt, width), edge_ref[e].astype(f32), 0.0)
                edge_buf[e, gx] = kept.astype(jnp.bfloat16)
        acc[...] = jnp.zeros(acc.shape, f32)
        ey[0, 0] = jnp.ones((TS, TS), f32)
        ey[0, 1] = jnp.zeros((TS, TS), f32)
        for n in range(1, HIGHEST_RY):
            r, i = ey[n - 1, 0], ey[n - 1, 1]
            a, b = wave_ref[0], wave_ref[1]
            ey[n, 0] = r * a - i * b
            ey[n, 1] = r * b + i * a

    def put(buf, at, z, rows):
        z = z.astype(jnp.bfloat16)
        for r in range(chunk):
            for p in range(2):
                buf[at + (slice(p * rows, (p + 1) * rows), slice(r * TS, (r + 1) * TS))] = z[
                    r * rows : (r + 1) * rows, p * TS : (p + 1) * TS
                ]

    def data(first, last):
        rows = last - first
        own = own_ref[:, first:last, :].reshape(chunk * rows, TS)
        got = got_ref[:, first:last, :].reshape(chunk * rows, TS)
        return jnp.concatenate([own, got], 1)

    def x_items(gx):
        def item(gy):
            first, last = ((0, HALF), (0, INNER), (HALF, INNER))[gy]
            z = jnp.dot(data(first, last), cols_buf[gy, gx], preferred_element_type=f32)
            if gy == 1:
                put(z_mid, (gx,), z, INNER)
            else:
                put(z_edge, (gy // 2, gx), z, HALF)

        return [functools.partial(item, gy) for gy in range(GY)]

    def y_items(gx):
        def item(gy, lanes, rows):
            if gy == 1:
                s = jnp.dot(mid_ref[rows], z_mid[gx, :, lanes], preferred_element_type=f32)
            else:
                s = jnp.dot(edge_buf[gy // 2, gx, rows], z_edge[gy // 2, gx, :, lanes], preferred_element_type=f32)
            s_buf[gx, gy, rows, lanes] = s

        return [
            functools.partial(item, gy, slice(at, at + 2 * TS), slice(part, part + TS))
            for gy in range(GY)
            for at in range(0, chunk * TS, 2 * TS)
            for part in (0, TS)
        ]

    def gain_parts(with_b):
        def part(r, at0):
            rows = slice(at0, at0 + 2 * ROW_BLOCK)
            at = step * chunk + r
            hr = filt_ref[r, 0, rows].astype(f32)
            hi = filt_ref[r, 1, rows].astype(f32)
            wr = weight_ref[0, shift_ref[member, 2, at]]
            wi = weight_ref[1, shift_ref[member, 2, at]]
            gains[r, 0, rows] = wr * hr - wi * hi
            gains[r, 1, rows] = wr * hi + wi * hr
            if with_b:
                keep = (at < plan.paired).astype(f32)
                vr = weight_ref[0, shift_ref[member, 3, at]] * keep
                vi = -weight_ref[1, shift_ref[member, 3, at]] * keep
                n = jnp.clip(shift_ref[member, 0, at], 0, HIGHEST_RY - 1)
                turn = shift_ref[member, 1, at] + RW // 2
                ex_r = row_ref[0, pl.ds(turn, 1), :]
                ex_i = row_ref[1, pl.ds(turn, 1), :]
                er = jnp.broadcast_to(vr * ex_r - vi * ex_i, (2 * ROW_BLOCK, TS))
                ei = jnp.broadcast_to(vr * ex_i + vi * ex_r, (2 * ROW_BLOCK, TS))
                yr = ey[n, 0, rows]
                yi = ey[n, 1, rows]
                pr = yr * er - yi * ei
                pi = yr * ei + yi * er
                gains[r, 2, rows] = pr * hr - pi * hi
                gains[r, 3, rows] = pr * hi + pi * hr

        starts = range(0, TS, 2 * ROW_BLOCK)
        return [functools.partial(part, r, at) for at in starts for r in range(chunk)]

    def gather_parts(gx, with_b):
        sums_n = 4 if with_b else 2

        def part(v):
            rows = slice(v * ROW_BLOCK, (v + 1) * ROW_BLOCK)
            low = slice(TS + v * ROW_BLOCK, TS + (v + 1) * ROW_BLOCK)
            sums = [[acc[gy, gx, c, rows] for c in range(sums_n)] for gy in range(GY)]
            for r in range(chunk):
                lanes = slice(r * TS, (r + 1) * TS)
                g = [gains[r, c, rows] for c in range(sums_n)]
                for gy in range(GY):
                    sr = s_buf[gx, gy, rows, lanes]
                    si = s_buf[gx, gy, low, lanes]
                    for c in range(0, sums_n, 2):
                        sums[gy][c] = sums[gy][c] + (g[c] * sr - g[c + 1] * si)
                        sums[gy][c + 1] = sums[gy][c + 1] + (g[c] * si + g[c + 1] * sr)
            for gy in range(GY):
                for c in range(sums_n):
                    acc[gy, gx, c, rows] = sums[gy][c]

        return [functools.partial(part, v) for v in range(TS // ROW_BLOCK)]

    def run(with_b):
        for part in gain_parts(with_b):
            part()
        for gx in range(GX):
            for item in x_items(gx):
                item()
        for item in y_items(0):
            item()
        for gx in range(GX):
            interleave(y_items(gx + 1) if gx + 1 < GX else [], gather_parts(gx, with_b))

    @pl.when(step == 0)
    def _():
        prepare()

    @pl.when(step < plan.paired_steps)
    def _():
        run(True)

    @pl.when(step >= plan.paired_steps)
    def _():
        run(False)

    @pl.when(step == plan.steps - 1)
    def _():
        canvas[...] = jnp.zeros(canvas.shape, f32)
        row = iota((TS, TS), 0)
        lane = iota((TS, TS), 1)
        for gy in range(GY):
            for gx in range(GX):
                ar, ai, br, bi = [acc[gy, gx, c] for c in range(4)]
                both = jnp.concatenate(
                    [jnp.concatenate([ar + br, ai + bi], 1), jnp.concatenate([ar - br, ai - bi], 1)], 0
                )
                half = jnp.dot(split(both, 1), inv_right_ref[...], preferred_element_type=f32)
                plus = jnp.concatenate([half[:TS, :TS], half[:TS, TS:]], 0)
                minus = jnp.concatenate([half[TS:, :TS], half[TS:, TS:]], 0)
                fr = jnp.dot(inv_left_ref[:TS], split(plus, 0), preferred_element_type=f32)
                fi = jnp.dot(inv_left_ref[TS:], split(minus, 0), preferred_element_type=f32)
                width = width_ref[band + gy, 2 * chip + gx]
                pc = phasor_ref[0, band + gy, 2 * chip + gx]
                ps = phasor_ref[1, band + gy, 2 * chip + gx]
                inside = in_window(row, width) & in_window(lane, width)
                placed = (jnp.where(inside, fr * pc - fi * ps, 0.0), jnp.where(inside, fr * ps + fi * pc, 0.0))
                start = MARGIN + gx * INNER
                shift = start % TS
                rows = slice(gy * INNER, gy * INNER + TS)
                for part in range(2):
                    turned = pltpu.roll(placed[part], shift, 1)
                    canvas[start // TS, part, rows] += jnp.where(lane >= shift, turned, 0.0)
                    canvas[start // TS + 1, part, rows] += jnp.where(lane >= shift, 0.0, turned)
        left_out[...] = canvas[0].astype(left_out.dtype)
        mid_out[...] = canvas[1]
        right_out[...] = canvas[2].astype(right_out.dtype)


def deconvolve(plan, place, widths, phasors, weights, own, got, filt):
    chunk = plan.chunk
    y = np.arange(INNER)
    index = np.arange(TS)
    mid = as_bf16(forward_left(y + MARGIN))
    edge = np.stack([as_bf16(forward_left(y[:HALF] + TS - HALF)), as_bf16(forward_left(y[:HALF]))])
    wave = np.stack([np.cos(2 * math.pi * index / TS), np.sin(2 * math.pi * index / TS)])
    wave = np.broadcast_to(wave[:, :, None], (2, TS, TS)).astype(np.float32)
    shifts = np.arange(RW) - RW // 2
    theta = 2.0 * math.pi * (shifts[:, None] * index[None, :] % TS) / TS
    row = np.stack([np.cos(theta), np.sin(theta)]).astype(np.float32)
    inv_right, inv_left = inverse_tables()
    rows = (GY + 1) * INNER
    edge_canvas = jax.ShapeDtypeStruct((2, rows, TS), jnp.bfloat16)
    feed = pl.BlockSpec((chunk, INNER, TS), lambda i: (i, 0, 0))
    return pl.pallas_call(
        functools.partial(decon_kernel, plan),
        out_shape=(edge_canvas, jax.ShapeDtypeStruct((2, rows, TS), jnp.float32), edge_canvas),
        grid=(plan.steps,),
        in_specs=[
            smem(),
            smem(),
            smem(),
            smem(),
            smem(),
            feed,
            feed,
            pl.BlockSpec((chunk, 2, TS, TS), lambda i: (i, 0, 0, 0)),
            full(GX, 2, TS, 2 * TS),
            full(2 * TS, 2 * INNER),
            full(2, 2 * TS, 2 * HALF),
            full(2, TS, TS),
            full(2, RW, TS),
            full(6 * TS, 2 * TS),
            full(2 * TS, 6 * TS),
        ],
        out_specs=(full(2, rows, TS),) * 3,
        scratch_shapes=[
            pltpu.VMEM((GY, GX, 2 * TS, 2 * TS), jnp.bfloat16),
            pltpu.VMEM((2, GX, 2 * TS, 2 * HALF), jnp.bfloat16),
            pltpu.VMEM((GY, GX, 4, TS, TS), jnp.float32),
            pltpu.VMEM((GX, 2 * INNER, chunk * TS), jnp.bfloat16),
            pltpu.VMEM((2, GX, 2 * HALF, chunk * TS), jnp.bfloat16),
            pltpu.VMEM((GX, GY, 2 * TS, chunk * TS), jnp.float32),
            pltpu.VMEM((HIGHEST_RY, 2, TS, TS), jnp.float32),
            pltpu.VMEM((chunk, 4, TS, TS), jnp.float32),
            pltpu.VMEM((3, 2, rows, TS), jnp.float32),
        ],
        compiler_params=pltpu.CompilerParams(vmem_limit_bytes=56 * MIB),
        name="deconvolve",
    )(
        place,
        widths,
        phasors,
        jnp.asarray(plan.shift_tables()),
        weights,
        own,
        got,
        filt,
        jnp.asarray(plan.scan_tables()),
        jnp.asarray(mid),
        jnp.asarray(edge),
        jnp.asarray(wave),
        jnp.asarray(row),
        jnp.asarray(table_terms(inv_right, 0)),
        jnp.asarray(table_terms(inv_left, 1)),
    )


def passed_along(value, axis, steps):
    count = lax.axis_size(axis)
    leading, last = (max(0, -steps), min(count, count - steps))
    if leading >= last:
        return jnp.zeros_like(value)
    return lax.ppermute(value, axis, [(source, source + steps) for source in range(leading, last)])


def gathered(value, axis):
    count = lax.axis_size(axis)
    copies = jnp.broadcast_to(value[None], (count,) + value.shape)
    taken = lax.all_to_all(copies, axis, split_axis=0, concat_axis=0, tiled=True)
    return jnp.transpose(taken, (1, 0, 2)).reshape(value.shape[0], count * value.shape[1])


def own_part(plan, value, member):
    count = lax.axis_size("tile")
    if plan.group != 2:
        return lax.psum_scatter(
            value, "tile", scatter_dimension=2, axis_index_groups=plan.groups(count), tiled=True
        )
    zero = jnp.zeros((), jnp.int32)
    size = value.shape[:2] + (plan.cols,)
    kept = lax.dynamic_slice(value, (zero, zero, member * plan.cols), size)
    sent = lax.dynamic_slice(value, (zero, zero, (1 - member) * plan.cols), size)
    return kept + lax.ppermute(sent, "tile", [(i, i ^ 1) for i in range(count)])


def coverage(widths, inner, row_start, rows, col_start, cols):
    bands_n, per_band = widths.shape
    flat = jnp.arange(bands_n * per_band, dtype=jnp.int32)
    tile_band = flat // per_band
    tile_col = flat % per_band
    width = widths.reshape(-1)
    row_ids = row_start + jnp.arange(rows, dtype=jnp.int32)
    col_ids = col_start + jnp.arange(cols, dtype=jnp.int32)
    row_in = (
        (row_ids[None, :] >= (tile_band * inner - width)[:, None])
        & (row_ids[None, :] < (tile_band * inner + inner + width)[:, None])
    ).astype(jnp.float32)
    col_in = (
        (col_ids[None, :] >= (tile_col * inner - width)[:, None])
        & (col_ids[None, :] < (tile_col * inner + inner + width)[:, None])
    ).astype(jnp.float32)
    return jnp.dot(row_in.T, col_in, precision=lax.Precision.HIGHEST)


def local(frames, probe, rho_weights, phase_offsets, margin_widths):
    band = lax.axis_index("band").astype(jnp.int32)
    column = lax.axis_index("tile").astype(jnp.int32)
    plan = Plan(frames.shape[1])
    member = column % plan.group
    side = member if plan.group == 2 else jnp.zeros((), jnp.int32)
    place = jnp.stack([band, column // plan.group, member, side])
    weights = gathered(rho_weights, "tile")
    widths = jnp.pad(margin_widths, 1)
    angle = phase_offsets.astype(jnp.float32) * (2.0 * math.pi / phase_steps)
    phasors = jnp.pad(jnp.stack([jnp.cos(angle), jnp.sin(angle)]), ((0, 0), (1, 1), (1, 1)))
    own, got = shared_spectra(plan, place, frames)
    filt = filters(plan, place, probe)
    left, mid, right = deconvolve(plan, place, widths, phasors, weights, own, got, filt)
    mid = mid + passed_along(left, "tile", -plan.group) + passed_along(right, "tile", plan.group)
    first = MARGIN + INNER
    sent = mid.astype(jnp.bfloat16)
    mine = (
        mid[:, first : first + INNER]
        + passed_along(sent[:, first + INNER : first + 2 * INNER], "band", 1)
        + passed_along(sent[:, MARGIN:first], "band", -1)
    )
    far_down = passed_along(sent[:, first + 2 * INNER :], "band", 2)
    far_up = passed_along(sent[:, :MARGIN], "band", -2)
    mine = mine + jnp.concatenate([far_down, far_up], 1)
    total = own_part(plan, mine, member)
    count = coverage(margin_widths, INNER, band * INNER, INNER, column * plan.cols, plan.cols)
    return total / count[None]


def solution(mesh):
    return jax.shard_map(
        local,
        mesh=mesh,
        in_specs=(P("band", "tile", None), P(), P(None, "tile"), P(), P()),
        out_specs=P(None, "band", "tile"),
        check_vma=False,
    )
```

```python
import functools
import math

import jax
import jax.numpy as jnp
import numpy as np
from jax import lax
from jax.experimental import pallas as pl
from jax.experimental.pallas import tpu as pltpu
from jax.sharding import PartitionSpec as P

DY = 32
DX = 32
RW = 16
TS = 128
MARGIN = 32
INNER = TS - 2 * MARGIN
HALF = INNER // 2
GY = 3
GX = 4
phase_steps = 1024.0

MIB = 1024 * 1024


class Plan:
    def __init__(self, cols, held):
        lo = -(RW // 2)
        paired, alone = [], []
        for ry in range(lo, lo + RW):
            for rx in range(lo, lo + RW):
                if ry == lo or rx == lo or (ry == 0 and rx == 0):
                    alone.append((ry, rx))
                elif ry > 0 or (ry == 0 and rx > 0):
                    paired.append((ry, rx))
        self.cols = cols
        self.held = held
        self.group = TS // cols
        self.lists = [paired[c :: self.group] + alone[c :: self.group] for c in range(self.group)]
        self.paired = len(paired) // self.group
        self.share = len(self.lists[0])
        self.chunk = 4 if self.share % 4 == 0 else 2
        self.steps = self.share // self.chunk
        self.paired_steps = -(-self.paired // self.chunk)

    def shift_tables(self):
        rows = np.zeros((self.group, 6, self.share), np.int32)
        for c in range(self.group):
            for i, (ry, rx) in enumerate(self.lists[c]):
                rows[c, 0, i] = ry
                rows[c, 1, i] = rx
                partner = rho_of(-ry, -rx) if i < self.paired else rho_of(ry, rx)
                rows[c, 2:4, i] = divmod(rho_of(ry, rx), self.held)
                rows[c, 4:6, i] = divmod(partner, self.held)
        return rows

    def groups(self, count):
        return [list(range(at, at + self.group)) for at in range(0, count, self.group)]

    def scan_tables(self):
        x = np.arange(self.cols)
        halves = []
        for gx in range(GX):
            rows = [forward_right(c * self.cols + x - (gx - 1) * INNER + MARGIN) for c in range(self.group)]
            halves.append(np.concatenate(rows).reshape(2, TS, 2 * TS))
        return as_bf16(np.stack(halves))


HIGHEST_RY = RW // 2


def rho_of(ry, rx):
    return (ry + RW // 2) * RW + rx + RW // 2


def detector_table(order):
    ky = np.arange(DY)
    kx = np.arange(DX)
    out = np.zeros((2, len(order), DY * DX), np.float64)
    for i, (ry, rx) in enumerate(order):
        turns = ((ry * ky) % DY)[:, None] / DY + ((rx * kx) % DX)[None, :] / DX
        theta = 2.0 * math.pi * turns.reshape(-1)
        out[0, i] = np.cos(theta)
        out[1, i] = np.sin(theta)
    return as_bf16(out.reshape(2 * len(order), DY * DX) / math.sqrt(DY * DX))


def waves():
    index = np.arange(TS)
    theta = 2.0 * math.pi * (index[:, None] * index[None, :] % TS) / TS
    return np.cos(theta) / math.sqrt(TS), np.sin(theta) / math.sqrt(TS)


def forward_right(positions):
    cosine, sine = waves()
    valid = ((positions >= 0) & (positions < TS)).astype(np.float64)[:, None]
    at = np.clip(positions, 0, TS - 1)
    c, s = cosine[at] * valid, sine[at] * valid
    return np.block([[c, -s], [s, c]])


def forward_left(positions):
    return forward_right(positions).T


def inverse_tables():
    cosine, sine = waves()
    right = np.block([[cosine, sine], [-sine, cosine]]).astype(np.float32)
    real = np.concatenate([cosine, -sine], 1).astype(np.float32)
    imag = np.concatenate([sine, cosine], 1).astype(np.float32)
    return right, np.concatenate([real, imag], 0)


def as_bf16(table):
    return table.astype(np.float32).astype(jnp.bfloat16)


def iota(shape, dim):
    return lax.broadcasted_iota(jnp.int32, shape, dim)


ROWS_AT_ONCE = 16


def detector_kernel(table_ref, frames_ref, own_ref, other_ref, buf):
    share = own_ref.shape[0]
    both = 2 * share
    table = table_ref[0]
    lane = iota((both, TS), 1)
    low = lane < INNER
    for part in range(2):
        rows = ROWS_AT_ONCE // 2
        block = frames_ref[part * rows : (part + 1) * rows].reshape(rows * INNER, DY * DX)
        out = lax.dot_general(table, block, (((1,), (1,)), ((), ())), preferred_element_type=jnp.float32)
        for pair in range(rows // 2):
            c = out[:both, pair * TS : (pair + 1) * TS]
            s = out[both:, pair * TS : (pair + 1) * TS]
            first = jnp.where(low, c, pltpu.roll(s, INNER, 1))
            second = jnp.where(low, pltpu.roll(c, INNER, 1), s)
            y = part * rows + pair * 2
            buf[pl.ds(y, both, stride=ROWS_AT_ONCE), :] = first
            buf[pl.ds(y + 1, both, stride=ROWS_AT_ONCE), :] = second
    own_ref[...] = buf[: share * ROWS_AT_ONCE].reshape(share, ROWS_AT_ONCE, TS).astype(jnp.bfloat16)
    other_ref[...] = buf[share * ROWS_AT_ONCE :].reshape(share, ROWS_AT_ONCE, TS).astype(jnp.bfloat16)


def detector(plan, place, frames):
    share = plan.share
    tables = jnp.asarray(np.stack([detector_table(plan.lists[c] + plan.lists[1 - c]) for c in range(2)]))
    shape = jax.ShapeDtypeStruct((share, INNER, TS), jnp.bfloat16)
    spec = pl.BlockSpec((share, ROWS_AT_ONCE, TS), lambda i, place: (0, i, 0))

    def body(place_ref, *refs):
        detector_kernel(*refs)

    return pl.pallas_call(
        body,
        out_shape=(shape, shape),
        grid_spec=pltpu.PrefetchScalarGridSpec(
            num_scalar_prefetch=1,
            grid=(INNER // ROWS_AT_ONCE,),
            in_specs=[
                pl.BlockSpec((1, 4 * share, DY * DX), lambda i, place: (place[2], 0, 0)),
                pl.BlockSpec((ROWS_AT_ONCE, INNER, DY * DX), lambda i, place: (i, 0, 0)),
            ],
            out_specs=[spec, spec],
            scratch_shapes=[pltpu.VMEM((2 * share * ROWS_AT_ONCE, TS), jnp.float32)],
        ),
        compiler_params=pltpu.CompilerParams(vmem_limit_bytes=58 * MIB),
        name="detector",
    )(place, tables, frames)


def detector_any(plan, frames):
    rows, cols, pixels = frames.shape
    table = detector_table([rho for part in plan.lists for rho in part])
    spectra = lax.dot_general(
        jnp.asarray(table),
        frames.reshape(rows * cols, pixels),
        (((1,), (1,)), ((), ())),
        preferred_element_type=jnp.float32,
    ).astype(jnp.bfloat16)
    spectra = spectra.reshape(2, plan.group, plan.share, rows, cols)
    return jnp.transpose(spectra, (1, 2, 3, 0, 4)).reshape(plan.group, plan.share, rows, 2 * cols)


def shared_spectra(plan, place, frames):
    count = lax.axis_size("tile")
    if plan.group == 2:
        own, other = detector(plan, place, frames)
        return own, lax.ppermute(other, "tile", [(i, i ^ 1) for i in range(count)])
    spectra = detector_any(plan, frames)
    taken = lax.all_to_all(
        spectra, "tile", split_axis=0, concat_axis=0, axis_index_groups=plan.groups(count), tiled=True
    )
    taken = jnp.transpose(taken.reshape(2, plan.group // 2, plan.share, INNER, 2 * plan.cols), (0, 2, 3, 1, 4))
    taken = taken.reshape(2, plan.share, INNER, TS)
    return taken[0], taken[1]


ROW_BLOCK = 8


def filter_kernel(plan, place_ref, shift_ref, probe_ref, right_ref, left_ref, out_ref, first_buf, stack_buf, chi_buf):
    member = place_ref[2]
    step = pl.program_id(0)
    chunk = plan.chunk
    for pair in range(0, chunk, 2):
        lanes = slice(pair * TS, (pair + 2) * TS)
        for part in range(2):
            rows = slice(part * TS, (part + 1) * TS)
            chi_buf[rows, lanes] = jnp.dot(left_ref[rows], stack_buf[:, lanes], preferred_element_type=jnp.float32)
    for r in range(chunk):
        lanes = slice(r * TS, (r + 1) * TS)
        for start in range(0, TS, 2 * ROW_BLOCK):
            cr = chi_buf[start : start + 2 * ROW_BLOCK, lanes]
            ci = chi_buf[TS + start : TS + start + 2 * ROW_BLOCK, lanes]
            inv = 1.0 / (cr * cr + ci * ci + 1.0)
            out_ref[r, 0, start : start + 2 * ROW_BLOCK] = (cr * inv).astype(jnp.bfloat16)
            out_ref[r, 1, start : start + 2 * ROW_BLOCK] = (-ci * inv).astype(jnp.bfloat16)
    base_r, base_i = probe_ref[0], probe_ref[1]
    for r in range(chunk):
        at = jnp.minimum(step * chunk + r, plan.share - 1)
        back_y = lax.rem(TS - shift_ref[member, 0, at], TS)
        back_x = lax.rem(TS - shift_ref[member, 1, at], TS)
        moved_r = pltpu.roll(pltpu.roll(base_r, back_y, 0), back_x, 1)
        moved_i = pltpu.roll(pltpu.roll(base_i, back_y, 0), back_x, 1)
        real = base_r * moved_r + base_i * moved_i
        imag = base_i * moved_r - base_r * moved_i
        first_buf[r, :, :TS] = real.astype(jnp.bfloat16)
        first_buf[r, :, TS:] = imag.astype(jnp.bfloat16)
        middle = jnp.dot(first_buf[r], right_ref[...], preferred_element_type=jnp.float32).astype(jnp.bfloat16)
        for p in range(2):
            stack_buf[p * TS : (p + 1) * TS, r * TS : (r + 1) * TS] = middle[:, p * TS : (p + 1) * TS]


def smem():
    return pl.BlockSpec(memory_space=pltpu.SMEM)


def full(*shape):
    return pl.BlockSpec(shape, lambda i: (0,) * len(shape))


def filters(plan, place, probe):
    chunk = plan.chunk
    right = forward_right(np.arange(TS))
    return pl.pallas_call(
        functools.partial(filter_kernel, plan),
        out_shape=jax.ShapeDtypeStruct((plan.share, 2, TS, TS), jnp.bfloat16),
        grid=(plan.steps + 1,),
        in_specs=[smem(), smem(), full(2, TS, TS), full(2 * TS, 2 * TS), full(2 * TS, 2 * TS)],
        out_specs=pl.BlockSpec((chunk, 2, TS, TS), lambda i: (jnp.maximum(i - 1, 0), 0, 0, 0)),
        scratch_shapes=[
            pltpu.VMEM((chunk, TS, 2 * TS), jnp.bfloat16),
            pltpu.VMEM((2 * TS, chunk * TS), jnp.bfloat16),
            pltpu.VMEM((2 * TS, chunk * TS), jnp.float32),
        ],
        compiler_params=pltpu.CompilerParams(vmem_limit_bytes=58 * MIB),
        name="filters",
    )(place, jnp.asarray(plan.shift_tables()), probe, jnp.asarray(as_bf16(right)), jnp.asarray(as_bf16(right.T)))


def in_window(index, width):
    return (index >= MARGIN - width) & (index < TS - MARGIN + width)


def split(value, axis):
    high = value.astype(jnp.bfloat16)
    low = (value - high.astype(jnp.float32)).astype(jnp.bfloat16)
    return jnp.concatenate([high, low, high], axis)


def table_terms(table, axis):
    high = as_bf16(table)
    low = as_bf16(table - high.astype(np.float64))
    return np.concatenate([high, high, low], axis)


def interleave(items, parts):
    done = 0
    for i, part in enumerate(parts):
        while done < len(items) and done * len(parts) <= i * len(items):
            items[done]()
            done += 1
        part()
    for item in items[done:]:
        item()


def decon_kernel(plan, place_ref, width_ref, phasor_ref, shift_ref, weight_ref, own_ref, got_ref, filt_ref,
                 cols_ref, mid_ref, edge_ref, wave_ref, row_ref, inv_right_ref, inv_left_ref,
                 left_out, mid_out, right_out,
                 cols_buf, edge_buf, acc, z_mid, z_edge, s_buf, ey, gains, canvas):
    step = pl.program_id(0)
    band = place_ref[0]
    chip = place_ref[1]
    member = place_ref[2]
    side_first = place_ref[3]
    chunk = plan.chunk
    f32 = jnp.float32

    def tile_at(gy, gx):
        bands, columns = width_ref.shape
        row = band + gy - 1
        column = 2 * chip + gx - 1
        real = (row >= 0) & (row < bands) & (column >= 0) & (column < columns)
        return jnp.clip(row, 0, bands - 1), jnp.clip(column, 0, columns - 1), real.astype(f32)

    def width_of(gy, gx):
        row, column, _ = tile_at(gy, gx)
        return width_ref[row, column]

    def prepare():
        row = iota((TS, 2 * TS), 0)
        x = row // (2 * plan.cols) * plan.cols + row % plan.cols
        lane = iota((2 * TS, 2 * HALF), 1)
        y = jnp.where(lane < HALF, lane, lane - HALF)
        for gx in range(GX):
            for o in range(2):
                side = side_first if o == 0 else 1 - side_first
                table = cols_ref[gx, pl.ds(side, 1)][0].astype(f32)
                xt = side * INNER + x - (gx - 1) * INNER + MARGIN
                for gy in range(GY):
                    width = width_of(gy, gx)
                    kept = jnp.where(in_window(xt, width), table, 0.0)
                    cols_buf[gy, gx, o * TS : (o + 1) * TS] = kept.astype(jnp.bfloat16)
            for e in range(2):
                width = width_of(2 * e, gx)
                yt = y + (TS - HALF if e == 0 else 0)
                kept = jnp.where(in_window(yt, width), edge_ref[e].astype(f32), 0.0)
                edge_buf[e, gx] = kept.astype(jnp.bfloat16)
        acc[...] = jnp.zeros(acc.shape, f32)
        ey[0, 0] = jnp.ones((TS, TS), f32)
        ey[0, 1] = jnp.zeros((TS, TS), f32)
        for n in range(1, HIGHEST_RY):
            r, i = ey[n - 1, 0], ey[n - 1, 1]
            a, b = wave_ref[0], wave_ref[1]
            ey[n, 0] = r * a - i * b
            ey[n, 1] = r * b + i * a

    def put(buf, at, z, rows):
        z = z.astype(jnp.bfloat16)
        for r in range(chunk):
            for p in range(2):
                buf[at + (slice(p * rows, (p + 1) * rows), slice(r * TS, (r + 1) * TS))] = z[
                    r * rows : (r + 1) * rows, p * TS : (p + 1) * TS
                ]

    def data(first, last):
        rows = last - first
        own = own_ref[:, first:last, :].reshape(chunk * rows, TS)
        got = got_ref[:, first:last, :].reshape(chunk * rows, TS)
        return jnp.concatenate([own, got], 1)

    def x_items(gx):
        def item(gy):
            first, last = ((0, HALF), (0, INNER), (HALF, INNER))[gy]
            z = jnp.dot(data(first, last), cols_buf[gy, gx], preferred_element_type=f32)
            if gy == 1:
                put(z_mid, (gx,), z, INNER)
            else:
                put(z_edge, (gy // 2, gx), z, HALF)

        return [functools.partial(item, gy) for gy in range(GY)]

    def y_items(gx):
        def item(gy, lanes, rows):
            if gy == 1:
                s = jnp.dot(mid_ref[rows], z_mid[gx, :, lanes], preferred_element_type=f32)
            else:
                s = jnp.dot(edge_buf[gy // 2, gx, rows], z_edge[gy // 2, gx, :, lanes], preferred_element_type=f32)
            s_buf[gx, gy, rows, lanes] = s

        return [
            functools.partial(item, gy, slice(at, at + 2 * TS), slice(part, part + TS))
            for gy in range(GY)
            for at in range(0, chunk * TS, 2 * TS)
            for part in (0, TS)
        ]

    def gain_parts(with_b):
        def part(r, at0):
            rows = slice(at0, at0 + 2 * ROW_BLOCK)
            at = step * chunk + r
            hr = filt_ref[r, 0, rows].astype(f32)
            hi = filt_ref[r, 1, rows].astype(f32)
            wr = weight_ref[shift_ref[member, 2, at], 0, shift_ref[member, 3, at]]
            wi = weight_ref[shift_ref[member, 2, at], 1, shift_ref[member, 3, at]]
            gains[r, 0, rows] = wr * hr - wi * hi
            gains[r, 1, rows] = wr * hi + wi * hr
            if with_b:
                keep = (at < plan.paired).astype(f32)
                vr = weight_ref[shift_ref[member, 4, at], 0, shift_ref[member, 5, at]] * keep
                vi = -weight_ref[shift_ref[member, 4, at], 1, shift_ref[member, 5, at]] * keep
                n = jnp.clip(shift_ref[member, 0, at], 0, HIGHEST_RY - 1)
                turn = shift_ref[member, 1, at] + RW // 2
                ex_r = row_ref[0, pl.ds(turn, 1), :]
                ex_i = row_ref[1, pl.ds(turn, 1), :]
                er = jnp.broadcast_to(vr * ex_r - vi * ex_i, (2 * ROW_BLOCK, TS))
                ei = jnp.broadcast_to(vr * ex_i + vi * ex_r, (2 * ROW_BLOCK, TS))
                yr = ey[n, 0, rows]
                yi = ey[n, 1, rows]
                pr = yr * er - yi * ei
                pi = yr * ei + yi * er
                gains[r, 2, rows] = pr * hr - pi * hi
                gains[r, 3, rows] = pr * hi + pi * hr

        starts = range(0, TS, 2 * ROW_BLOCK)
        return [functools.partial(part, r, at) for at in starts for r in range(chunk)]

    def gather_parts(gx, with_b):
        sums_n = 4 if with_b else 2

        def part(v):
            rows = slice(v * ROW_BLOCK, (v + 1) * ROW_BLOCK)
            low = slice(TS + v * ROW_BLOCK, TS + (v + 1) * ROW_BLOCK)
            sums = [[acc[gy, gx, c, rows] for c in range(sums_n)] for gy in range(GY)]
            for r in range(chunk):
                lanes = slice(r * TS, (r + 1) * TS)
                g = [gains[r, c, rows] for c in range(sums_n)]
                for gy in range(GY):
                    sr = s_buf[gx, gy, rows, lanes]
                    si = s_buf[gx, gy, low, lanes]
                    for c in range(0, sums_n, 2):
                        sums[gy][c] = sums[gy][c] + (g[c] * sr - g[c + 1] * si)
                        sums[gy][c + 1] = sums[gy][c + 1] + (g[c] * si + g[c + 1] * sr)
            for gy in range(GY):
                for c in range(sums_n):
                    acc[gy, gx, c, rows] = sums[gy][c]

        return [functools.partial(part, v) for v in range(TS // ROW_BLOCK)]

    def run(with_b):
        for part in gain_parts(with_b):
            part()
        for gx in range(GX):
            for item in x_items(gx):
                item()
        for item in y_items(0):
            item()
        for gx in range(GX):
            interleave(y_items(gx + 1) if gx + 1 < GX else [], gather_parts(gx, with_b))

    @pl.when(step == 0)
    def _():
        prepare()

    @pl.when(step < plan.paired_steps)
    def _():
        run(True)

    @pl.when(step >= plan.paired_steps)
    def _():
        run(False)

    @pl.when(step == plan.steps - 1)
    def _():
        canvas[...] = jnp.zeros(canvas.shape, f32)
        row = iota((TS, TS), 0)
        lane = iota((TS, TS), 1)
        for gy in range(GY):
            for gx in range(GX):
                ar, ai, br, bi = [acc[gy, gx, c] for c in range(4)]
                both = jnp.concatenate(
                    [jnp.concatenate([ar + br, ai + bi], 1), jnp.concatenate([ar - br, ai - bi], 1)], 0
                )
                half = jnp.dot(split(both, 1), inv_right_ref[...], preferred_element_type=f32)
                plus = jnp.concatenate([half[:TS, :TS], half[:TS, TS:]], 0)
                minus = jnp.concatenate([half[TS:, :TS], half[TS:, TS:]], 0)
                fr = jnp.dot(inv_left_ref[:TS], split(plus, 0), preferred_element_type=f32)
                fi = jnp.dot(inv_left_ref[TS:], split(minus, 0), preferred_element_type=f32)
                band_at, column_at, there = tile_at(gy, gx)
                width = width_ref[band_at, column_at]
                pc = phasor_ref[0, band_at, column_at] * there
                ps = phasor_ref[1, band_at, column_at] * there
                inside = in_window(row, width) & in_window(lane, width)
                placed = (jnp.where(inside, fr * pc - fi * ps, 0.0), jnp.where(inside, fr * ps + fi * pc, 0.0))
                start = MARGIN + gx * INNER
                shift = start % TS
                rows = slice(gy * INNER, gy * INNER + TS)
                for part in range(2):
                    turned = pltpu.roll(placed[part], shift, 1)
                    canvas[start // TS, part, rows] += jnp.where(lane >= shift, turned, 0.0)
                    canvas[start // TS + 1, part, rows] += jnp.where(lane >= shift, 0.0, turned)
        left_out[...] = canvas[0].astype(left_out.dtype)
        mid_out[...] = canvas[1]
        right_out[...] = canvas[2].astype(right_out.dtype)


def deconvolve(plan, place, widths, phasors, weights, own, got, filt):
    chunk = plan.chunk
    y = np.arange(INNER)
    index = np.arange(TS)
    mid = as_bf16(forward_left(y + MARGIN))
    edge = np.stack([as_bf16(forward_left(y[:HALF] + TS - HALF)), as_bf16(forward_left(y[:HALF]))])
    wave = np.stack([np.cos(2 * math.pi * index / TS), np.sin(2 * math.pi * index / TS)])
    wave = np.broadcast_to(wave[:, :, None], (2, TS, TS)).astype(np.float32)
    shifts = np.arange(RW) - RW // 2
    theta = 2.0 * math.pi * (shifts[:, None] * index[None, :] % TS) / TS
    row = np.stack([np.cos(theta), np.sin(theta)]).astype(np.float32)
    inv_right, inv_left = inverse_tables()
    rows = (GY + 1) * INNER
    edge_canvas = jax.ShapeDtypeStruct((2, rows, TS), jnp.bfloat16)
    feed = pl.BlockSpec((chunk, INNER, TS), lambda i: (i, 0, 0))
    return pl.pallas_call(
        functools.partial(decon_kernel, plan),
        out_shape=(edge_canvas, jax.ShapeDtypeStruct((2, rows, TS), jnp.float32), edge_canvas),
        grid=(plan.steps,),
        in_specs=[
            smem(),
            smem(),
            smem(),
            smem(),
            smem(),
            feed,
            feed,
            pl.BlockSpec((chunk, 2, TS, TS), lambda i: (i, 0, 0, 0)),
            full(GX, 2, TS, 2 * TS),
            full(2 * TS, 2 * INNER),
            full(2, 2 * TS, 2 * HALF),
            full(2, TS, TS),
            full(2, RW, TS),
            full(6 * TS, 2 * TS),
            full(2 * TS, 6 * TS),
        ],
        out_specs=(full(2, rows, TS),) * 3,
        scratch_shapes=[
            pltpu.VMEM((GY, GX, 2 * TS, 2 * TS), jnp.bfloat16),
            pltpu.VMEM((2, GX, 2 * TS, 2 * HALF), jnp.bfloat16),
            pltpu.VMEM((GY, GX, 4, TS, TS), jnp.float32),
            pltpu.VMEM((GX, 2 * INNER, chunk * TS), jnp.bfloat16),
            pltpu.VMEM((2, GX, 2 * HALF, chunk * TS), jnp.bfloat16),
            pltpu.VMEM((GX, GY, 2 * TS, chunk * TS), jnp.float32),
            pltpu.VMEM((HIGHEST_RY, 2, TS, TS), jnp.float32),
            pltpu.VMEM((chunk, 4, TS, TS), jnp.float32),
            pltpu.VMEM((3, 2, rows, TS), jnp.float32),
        ],
        compiler_params=pltpu.CompilerParams(vmem_limit_bytes=58 * MIB),
        name="deconvolve",
    )(
        place,
        widths,
        phasors,
        jnp.asarray(plan.shift_tables()),
        weights,
        own,
        got,
        filt,
        jnp.asarray(plan.scan_tables()),
        jnp.asarray(mid),
        jnp.asarray(edge),
        jnp.asarray(wave),
        jnp.asarray(row),
        jnp.asarray(table_terms(inv_right, 0)),
        jnp.asarray(table_terms(inv_left, 1)),
    )


def passed_along(value, axis, steps):
    count = lax.axis_size(axis)
    leading, last = (max(0, -steps), min(count, count - steps))
    if leading >= last:
        return jnp.zeros_like(value)
    return lax.ppermute(value, axis, [(source, source + steps) for source in range(leading, last)])


def gathered(value, axis):
    count = lax.axis_size(axis)
    copies = jnp.broadcast_to(value[None], (count,) + value.shape)
    return lax.all_to_all(copies, axis, split_axis=0, concat_axis=0, tiled=True)


def own_rows(value):
    bands = lax.axis_size("band")
    sent = value.astype(jnp.bfloat16)
    first = MARGIN + INNER
    if bands > 4:
        mine = (
            value[:, first : first + INNER]
            + passed_along(sent[:, first + INNER : first + 2 * INNER], "band", 1)
            + passed_along(sent[:, MARGIN:first], "band", -1)
        )
        far_down = passed_along(sent[:, first + 2 * INNER :], "band", 2)
        far_up = passed_along(sent[:, :MARGIN], "band", -2)
        return mine + jnp.concatenate([far_down, far_up], 1)
    zero = jnp.zeros((), jnp.int32)
    band = lax.axis_index("band").astype(jnp.int32)
    scan = jnp.zeros((2, (bands + 4) * INNER, TS), jnp.bfloat16)
    scan = lax.dynamic_update_slice(scan, sent, (zero, band * INNER + 2 * INNER - first, zero))
    scan = scan[:, 2 * INNER : (bands + 2) * INNER].reshape(2, bands, INNER, TS)
    taken = lax.all_to_all(scan, "band", split_axis=1, concat_axis=1, tiled=True)
    return jnp.sum(taken.astype(jnp.float32), 1)


def own_part(plan, value, member):
    count = lax.axis_size("tile")
    if plan.group != 2:
        return lax.psum_scatter(
            value, "tile", scatter_dimension=2, axis_index_groups=plan.groups(count), tiled=True
        )
    zero = jnp.zeros((), jnp.int32)
    size = value.shape[:2] + (plan.cols,)
    kept = lax.dynamic_slice(value, (zero, zero, member * plan.cols), size)
    sent = lax.dynamic_slice(value, (zero, zero, (1 - member) * plan.cols), size)
    return kept + lax.ppermute(sent, "tile", [(i, i ^ 1) for i in range(count)])


def coverage(widths, inner, row_start, rows, col_start, cols):
    bands_n, per_band = widths.shape
    flat = jnp.arange(bands_n * per_band, dtype=jnp.int32)
    tile_band = flat // per_band
    tile_col = flat % per_band
    width = widths.reshape(-1)
    row_ids = row_start + jnp.arange(rows, dtype=jnp.int32)
    col_ids = col_start + jnp.arange(cols, dtype=jnp.int32)
    row_in = (
        (row_ids[None, :] >= (tile_band * inner - width)[:, None])
        & (row_ids[None, :] < (tile_band * inner + inner + width)[:, None])
    ).astype(jnp.float32)
    col_in = (
        (col_ids[None, :] >= (tile_col * inner - width)[:, None])
        & (col_ids[None, :] < (tile_col * inner + inner + width)[:, None])
    ).astype(jnp.float32)
    return jnp.dot(row_in.T, col_in, precision=lax.Precision.HIGHEST)


def local(frames, probe, rho_weights, phase_offsets, margin_widths):
    band = lax.axis_index("band").astype(jnp.int32)
    column = lax.axis_index("tile").astype(jnp.int32)
    plan = Plan(frames.shape[1], rho_weights.shape[1])
    member = column % plan.group
    side = member if plan.group == 2 else jnp.zeros((), jnp.int32)
    place = jnp.stack([band, column // plan.group, member, side])
    weights = gathered(rho_weights, "tile")
    angle = phase_offsets.astype(jnp.float32) * (2.0 * math.pi / phase_steps)
    phasors = jnp.stack([jnp.cos(angle), jnp.sin(angle)])
    own, got = shared_spectra(plan, place, frames)
    filt = filters(plan, place, probe)
    left, mid, right = deconvolve(plan, place, margin_widths, phasors, weights, own, got, filt)
    mid = mid + passed_along(left, "tile", -plan.group) + passed_along(right, "tile", plan.group)
    mine = own_rows(mid)
    total = own_part(plan, mine, member)
    count = coverage(margin_widths, INNER, band * INNER, INNER, column * plan.cols, plan.cols)
    return total / count[None]


def solution(mesh):
    return jax.shard_map(
        local,
        mesh=mesh,
        in_specs=(P("band", "tile", None), P(), P(None, "tile"), P(), P()),
        out_specs=P(None, "band", "tile"),
        check_vma=False,
    )
```

```python
import functools
import math

import jax
import jax.numpy as jnp
import numpy as np
from jax import lax
from jax.experimental import pallas as pl
from jax.experimental.pallas import tpu as pltpu
from jax.sharding import PartitionSpec as P

DY = 32
DX = 32
RW = 16
TS = 128
MARGIN = 32
INNER = TS - 2 * MARGIN
HALF = INNER // 2
GY = 3
GX = 4
phase_steps = 1024.0

MIB = 1024 * 1024


class Plan:
    def __init__(self, cols, held):
        lo = -(RW // 2)
        paired, alone = [], []
        for ry in range(lo, lo + RW):
            for rx in range(lo, lo + RW):
                if ry == lo or rx == lo or (ry == 0 and rx == 0):
                    alone.append((ry, rx))
                elif ry > 0 or (ry == 0 and rx > 0):
                    paired.append((ry, rx))
        self.cols = cols
        self.held = held
        self.group = TS // cols
        self.lists = [paired[c :: self.group] + alone[c :: self.group] for c in range(self.group)]
        self.paired = len(paired) // self.group
        self.share = len(self.lists[0])
        self.chunk = 4 if self.share % 4 == 0 else 2
        self.steps = self.share // self.chunk
        self.paired_steps = -(-self.paired // self.chunk)

    def shift_tables(self):
        rows = np.zeros((self.group, 6, self.share), np.int32)
        for c in range(self.group):
            for i, (ry, rx) in enumerate(self.lists[c]):
                rows[c, 0, i] = ry
                rows[c, 1, i] = rx
                partner = rho_of(-ry, -rx) if i < self.paired else rho_of(ry, rx)
                rows[c, 2:4, i] = divmod(rho_of(ry, rx), self.held)
                rows[c, 4:6, i] = divmod(partner, self.held)
        return rows

    def groups(self, count):
        return [list(range(at, at + self.group)) for at in range(0, count, self.group)]

    def scan_tables(self):
        x = np.arange(self.cols)
        halves = []
        for gx in range(GX):
            rows = [forward_right(c * self.cols + x - (gx - 1) * INNER + MARGIN) for c in range(self.group)]
            halves.append(np.concatenate(rows).reshape(2, TS, 2 * TS))
        return as_bf16(np.stack(halves))


HIGHEST_RY = RW // 2


def rho_of(ry, rx):
    return (ry + RW // 2) * RW + rx + RW // 2


def detector_table(order):
    ky = np.arange(DY)
    kx = np.arange(DX)
    out = np.zeros((2, len(order), DY * DX), np.float64)
    for i, (ry, rx) in enumerate(order):
        turns = ((ry * ky) % DY)[:, None] / DY + ((rx * kx) % DX)[None, :] / DX
        theta = 2.0 * math.pi * turns.reshape(-1)
        out[0, i] = np.cos(theta)
        out[1, i] = np.sin(theta)
    return as_bf16(out.reshape(2 * len(order), DY * DX) / math.sqrt(DY * DX))


def waves():
    index = np.arange(TS)
    theta = 2.0 * math.pi * (index[:, None] * index[None, :] % TS) / TS
    return np.cos(theta) / math.sqrt(TS), np.sin(theta) / math.sqrt(TS)


def forward_right(positions):
    cosine, sine = waves()
    valid = ((positions >= 0) & (positions < TS)).astype(np.float64)[:, None]
    at = np.clip(positions, 0, TS - 1)
    c, s = cosine[at] * valid, sine[at] * valid
    return np.block([[c, -s], [s, c]])


def forward_left(positions):
    return forward_right(positions).T


def inverse_tables():
    cosine, sine = waves()
    right = np.block([[cosine, sine], [-sine, cosine]]).astype(np.float32)
    real = np.concatenate([cosine, -sine], 1).astype(np.float32)
    imag = np.concatenate([sine, cosine], 1).astype(np.float32)
    return right, np.concatenate([real, imag], 0)


def as_bf16(table):
    return table.astype(np.float32).astype(jnp.bfloat16)


def iota(shape, dim):
    return lax.broadcasted_iota(jnp.int32, shape, dim)


ROWS_AT_ONCE = 16


def detector_kernel(table_ref, frames_ref, own_ref, other_ref, buf):
    share = own_ref.shape[0]
    both = 2 * share
    table = table_ref[0]
    lane = iota((both, TS), 1)
    low = lane < INNER
    for part in range(2):
        rows = ROWS_AT_ONCE // 2
        block = frames_ref[part * rows : (part + 1) * rows].reshape(rows * INNER, DY * DX)
        out = lax.dot_general(table, block, (((1,), (1,)), ((), ())), preferred_element_type=jnp.float32)
        for pair in range(rows // 2):
            c = out[:both, pair * TS : (pair + 1) * TS]
            s = out[both:, pair * TS : (pair + 1) * TS]
            first = jnp.where(low, c, pltpu.roll(s, INNER, 1))
            second = jnp.where(low, pltpu.roll(c, INNER, 1), s)
            y = part * rows + pair * 2
            buf[pl.ds(y, both, stride=ROWS_AT_ONCE), :] = first
            buf[pl.ds(y + 1, both, stride=ROWS_AT_ONCE), :] = second
    own_ref[...] = buf[: share * ROWS_AT_ONCE].reshape(share, ROWS_AT_ONCE, TS).astype(jnp.bfloat16)
    other_ref[...] = buf[share * ROWS_AT_ONCE :].reshape(share, ROWS_AT_ONCE, TS).astype(jnp.bfloat16)


def detector(plan, place, frames):
    share = plan.share
    tables = jnp.asarray(np.stack([detector_table(plan.lists[c] + plan.lists[1 - c]) for c in range(2)]))
    shape = jax.ShapeDtypeStruct((share, INNER, TS), jnp.bfloat16)
    spec = pl.BlockSpec((share, ROWS_AT_ONCE, TS), lambda i, place: (0, i, 0))

    def body(place_ref, *refs):
        detector_kernel(*refs)

    return pl.pallas_call(
        body,
        out_shape=(shape, shape),
        grid_spec=pltpu.PrefetchScalarGridSpec(
            num_scalar_prefetch=1,
            grid=(INNER // ROWS_AT_ONCE,),
            in_specs=[
                pl.BlockSpec((1, 4 * share, DY * DX), lambda i, place: (place[2], 0, 0)),
                pl.BlockSpec((ROWS_AT_ONCE, INNER, DY * DX), lambda i, place: (i, 0, 0)),
            ],
            out_specs=[spec, spec],
            scratch_shapes=[pltpu.VMEM((2 * share * ROWS_AT_ONCE, TS), jnp.float32)],
        ),
        compiler_params=pltpu.CompilerParams(vmem_limit_bytes=58 * MIB),
        name="detector",
    )(place, tables, frames)


def detector_any(plan, frames):
    rows, cols, pixels = frames.shape
    table = detector_table([rho for part in plan.lists for rho in part])
    spectra = lax.dot_general(
        jnp.asarray(table),
        frames.reshape(rows * cols, pixels),
        (((1,), (1,)), ((), ())),
        preferred_element_type=jnp.float32,
    ).astype(jnp.bfloat16)
    spectra = spectra.reshape(2, plan.group, plan.share, rows, cols)
    return jnp.transpose(spectra, (1, 2, 3, 0, 4)).reshape(plan.group, plan.share, rows, 2 * cols)


def shared_spectra(plan, place, frames):
    count = lax.axis_size("tile")
    if plan.group == 2:
        own, other = detector(plan, place, frames)
        return own, lax.ppermute(other, "tile", [(i, i ^ 1) for i in range(count)])
    spectra = detector_any(plan, frames)
    taken = lax.all_to_all(
        spectra, "tile", split_axis=0, concat_axis=0, axis_index_groups=plan.groups(count), tiled=True
    )
    taken = jnp.transpose(taken.reshape(2, plan.group // 2, plan.share, INNER, 2 * plan.cols), (0, 2, 3, 1, 4))
    taken = taken.reshape(2, plan.share, INNER, TS)
    return taken[0], taken[1]


ROW_BLOCK = 8


def filter_kernel(plan, place_ref, shift_ref, probe_ref, right_ref, left_ref, out_ref, first_buf, stack_buf, chi_buf):
    member = place_ref[2]
    step = pl.program_id(0)
    chunk = plan.chunk
    for pair in range(0, chunk, 2):
        lanes = slice(pair * TS, (pair + 2) * TS)
        for part in range(2):
            rows = slice(part * TS, (part + 1) * TS)
            chi_buf[rows, lanes] = jnp.dot(left_ref[rows], stack_buf[:, lanes], preferred_element_type=jnp.float32)
    for r in range(chunk):
        lanes = slice(r * TS, (r + 1) * TS)
        for start in range(0, TS, 2 * ROW_BLOCK):
            cr = chi_buf[start : start + 2 * ROW_BLOCK, lanes]
            ci = chi_buf[TS + start : TS + start + 2 * ROW_BLOCK, lanes]
            inv = 1.0 / (cr * cr + ci * ci + 1.0)
            out_ref[r, 0, start : start + 2 * ROW_BLOCK] = (cr * inv).astype(jnp.bfloat16)
            out_ref[r, 1, start : start + 2 * ROW_BLOCK] = (-ci * inv).astype(jnp.bfloat16)
    base_r, base_i = probe_ref[0], probe_ref[1]
    for r in range(chunk):
        at = jnp.minimum(step * chunk + r, plan.share - 1)
        back_y = lax.rem(TS - shift_ref[member, 0, at], TS)
        back_x = lax.rem(TS - shift_ref[member, 1, at], TS)
        moved_r = pltpu.roll(pltpu.roll(base_r, back_y, 0), back_x, 1)
        moved_i = pltpu.roll(pltpu.roll(base_i, back_y, 0), back_x, 1)
        real = base_r * moved_r + base_i * moved_i
        imag = base_i * moved_r - base_r * moved_i
        first_buf[r, :, :TS] = real.astype(jnp.bfloat16)
        first_buf[r, :, TS:] = imag.astype(jnp.bfloat16)
        middle = jnp.dot(first_buf[r], right_ref[...], preferred_element_type=jnp.float32).astype(jnp.bfloat16)
        for p in range(2):
            stack_buf[p * TS : (p + 1) * TS, r * TS : (r + 1) * TS] = middle[:, p * TS : (p + 1) * TS]


def smem():
    return pl.BlockSpec(memory_space=pltpu.SMEM)


def full(*shape):
    return pl.BlockSpec(shape, lambda i: (0,) * len(shape))


def filters(plan, place, probe):
    chunk = plan.chunk
    right = forward_right(np.arange(TS))
    return pl.pallas_call(
        functools.partial(filter_kernel, plan),
        out_shape=jax.ShapeDtypeStruct((plan.share, 2, TS, TS), jnp.bfloat16),
        grid=(plan.steps + 1,),
        in_specs=[smem(), smem(), full(2, TS, TS), full(2 * TS, 2 * TS), full(2 * TS, 2 * TS)],
        out_specs=pl.BlockSpec((chunk, 2, TS, TS), lambda i: (jnp.maximum(i - 1, 0), 0, 0, 0)),
        scratch_shapes=[
            pltpu.VMEM((chunk, TS, 2 * TS), jnp.bfloat16),
            pltpu.VMEM((2 * TS, chunk * TS), jnp.bfloat16),
            pltpu.VMEM((2 * TS, chunk * TS), jnp.float32),
        ],
        compiler_params=pltpu.CompilerParams(vmem_limit_bytes=58 * MIB),
        name="filters",
    )(place, jnp.asarray(plan.shift_tables()), probe, jnp.asarray(as_bf16(right)), jnp.asarray(as_bf16(right.T)))


def in_window(index, width):
    return (index >= MARGIN - width) & (index < TS - MARGIN + width)


def interleave(items, parts):
    done = 0
    for i, part in enumerate(parts):
        while done < len(items) and done * len(parts) <= i * len(items):
            items[done]()
            done += 1
        part()
    for item in items[done:]:
        item()


def decon_kernel(plan, place_ref, width_ref, phasor_ref, shift_ref, weight_ref, own_ref, got_ref, filt_ref,
                 cols_ref, mid_ref, edge_ref, wave_ref, row_ref, inv_right_ref, inv_left_ref,
                 left_out, mid_out, right_out,
                 cols_buf, edge_buf, acc, z_mid, z_edge, s_buf, ey, gains, canvas):
    step = pl.program_id(0)
    band = place_ref[0]
    chip = place_ref[1]
    member = place_ref[2]
    side_first = place_ref[3]
    chunk = plan.chunk
    f32 = jnp.float32

    def tile_at(gy, gx):
        bands, columns = width_ref.shape
        row = band + gy - 1
        column = 2 * chip + gx - 1
        real = (row >= 0) & (row < bands) & (column >= 0) & (column < columns)
        return jnp.clip(row, 0, bands - 1), jnp.clip(column, 0, columns - 1), real.astype(f32)

    def width_of(gy, gx):
        row, column, _ = tile_at(gy, gx)
        return width_ref[row, column]

    def prepare():
        row = iota((TS, 2 * TS), 0)
        x = row // (2 * plan.cols) * plan.cols + row % plan.cols
        lane = iota((2 * TS, 2 * HALF), 1)
        y = jnp.where(lane < HALF, lane, lane - HALF)
        for gx in range(GX):
            for o in range(2):
                side = side_first if o == 0 else 1 - side_first
                table = cols_ref[gx, pl.ds(side, 1)][0].astype(f32)
                xt = side * INNER + x - (gx - 1) * INNER + MARGIN
                for gy in range(GY):
                    width = width_of(gy, gx)
                    kept = jnp.where(in_window(xt, width), table, 0.0)
                    cols_buf[gy, gx, o * TS : (o + 1) * TS] = kept.astype(jnp.bfloat16)
            for e in range(2):
                width = width_of(2 * e, gx)
                yt = y + (TS - HALF if e == 0 else 0)
                kept = jnp.where(in_window(yt, width), edge_ref[e].astype(f32), 0.0)
                edge_buf[e, gx] = kept.astype(jnp.bfloat16)
        acc[...] = jnp.zeros(acc.shape, f32)
        ey[0, 0] = jnp.ones((TS, TS), f32)
        ey[0, 1] = jnp.zeros((TS, TS), f32)
        for n in range(1, HIGHEST_RY):
            r, i = ey[n - 1, 0], ey[n - 1, 1]
            a, b = wave_ref[0], wave_ref[1]
            ey[n, 0] = r * a - i * b
            ey[n, 1] = r * b + i * a

    def put(buf, at, z, rows):
        z = z.astype(jnp.bfloat16)
        for r in range(chunk):
            for p in range(2):
                buf[at + (slice(p * rows, (p + 1) * rows), slice(r * TS, (r + 1) * TS))] = z[
                    r * rows : (r + 1) * rows, p * TS : (p + 1) * TS
                ]

    def data(first, last):
        rows = last - first
        own = own_ref[:, first:last, :].reshape(chunk * rows, TS)
        got = got_ref[:, first:last, :].reshape(chunk * rows, TS)
        return jnp.concatenate([own, got], 1)

    def x_items(gx):
        def item(gy):
            first, last = ((0, HALF), (0, INNER), (HALF, INNER))[gy]
            z = jnp.dot(data(first, last), cols_buf[gy, gx], preferred_element_type=f32)
            if gy == 1:
                put(z_mid, (gx,), z, INNER)
            else:
                put(z_edge, (gy // 2, gx), z, HALF)

        return [functools.partial(item, gy) for gy in range(GY)]

    def y_items(gx):
        def item(gy, lanes, rows):
            if gy == 1:
                s = jnp.dot(mid_ref[rows], z_mid[gx, :, lanes], preferred_element_type=f32)
            else:
                s = jnp.dot(edge_buf[gy // 2, gx, rows], z_edge[gy // 2, gx, :, lanes], preferred_element_type=f32)
            s_buf[gx, gy, rows, lanes] = s

        return [
            functools.partial(item, gy, slice(at, at + 2 * TS), slice(part, part + TS))
            for gy in range(GY)
            for at in range(0, chunk * TS, 2 * TS)
            for part in (0, TS)
        ]

    def gain_parts(with_b):
        def part(r, at0):
            rows = slice(at0, at0 + 2 * ROW_BLOCK)
            at = step * chunk + r
            hr = filt_ref[r, 0, rows].astype(f32)
            hi = filt_ref[r, 1, rows].astype(f32)
            wr = weight_ref[shift_ref[member, 2, at], 0, shift_ref[member, 3, at]]
            wi = weight_ref[shift_ref[member, 2, at], 1, shift_ref[member, 3, at]]
            gains[r, 0, rows] = wr * hr - wi * hi
            gains[r, 1, rows] = wr * hi + wi * hr
            if with_b:
                keep = (at < plan.paired).astype(f32)
                vr = weight_ref[shift_ref[member, 4, at], 0, shift_ref[member, 5, at]] * keep
                vi = -weight_ref[shift_ref[member, 4, at], 1, shift_ref[member, 5, at]] * keep
                n = jnp.clip(shift_ref[member, 0, at], 0, HIGHEST_RY - 1)
                turn = shift_ref[member, 1, at] + RW // 2
                ex_r = row_ref[0, pl.ds(turn, 1), :]
                ex_i = row_ref[1, pl.ds(turn, 1), :]
                er = jnp.broadcast_to(vr * ex_r - vi * ex_i, (2 * ROW_BLOCK, TS))
                ei = jnp.broadcast_to(vr * ex_i + vi * ex_r, (2 * ROW_BLOCK, TS))
                yr = ey[n, 0, rows]
                yi = ey[n, 1, rows]
                pr = yr * er - yi * ei
                pi = yr * ei + yi * er
                gains[r, 2, rows] = pr * hr - pi * hi
                gains[r, 3, rows] = pr * hi + pi * hr

        starts = range(0, TS, 2 * ROW_BLOCK)
        return [functools.partial(part, r, at) for at in starts for r in range(chunk)]

    def gather_parts(gx, with_b):
        sums_n = 4 if with_b else 2

        def part(v):
            rows = slice(v * ROW_BLOCK, (v + 1) * ROW_BLOCK)
            low = slice(TS + v * ROW_BLOCK, TS + (v + 1) * ROW_BLOCK)
            sums = [[acc[gy, gx, c, rows] for c in range(sums_n)] for gy in range(GY)]
            for r in range(chunk):
                lanes = slice(r * TS, (r + 1) * TS)
                g = [gains[r, c, rows] for c in range(sums_n)]
                for gy in range(GY):
                    sr = s_buf[gx, gy, rows, lanes]
                    si = s_buf[gx, gy, low, lanes]
                    for c in range(0, sums_n, 2):
                        sums[gy][c] = sums[gy][c] + (g[c] * sr - g[c + 1] * si)
                        sums[gy][c + 1] = sums[gy][c + 1] + (g[c] * si + g[c + 1] * sr)
            for gy in range(GY):
                for c in range(sums_n):
                    acc[gy, gx, c, rows] = sums[gy][c]

        return [functools.partial(part, v) for v in range(TS // ROW_BLOCK)]

    def run(with_b):
        for part in gain_parts(with_b):
            part()
        for gx in range(GX):
            for item in x_items(gx):
                item()
        for item in y_items(0):
            item()
        for gx in range(GX):
            interleave(y_items(gx + 1) if gx + 1 < GX else [], gather_parts(gx, with_b))

    @pl.when(step == 0)
    def _():
        prepare()

    @pl.when(step < plan.paired_steps)
    def _():
        run(True)

    @pl.when(step >= plan.paired_steps)
    def _():
        run(False)

    @pl.when(step == plan.steps - 1)
    def _():
        canvas[...] = jnp.zeros(canvas.shape, f32)
        row = iota((TS, TS), 0)
        lane = iota((TS, TS), 1)
        for gy in range(GY):
            for gx in range(GX):
                ar, ai, br, bi = [acc[gy, gx, c] for c in range(4)]
                plus = jnp.concatenate([ar + br, ai + bi], 1).astype(jnp.bfloat16)
                plus = jnp.dot(plus, inv_right_ref[...], preferred_element_type=f32).astype(jnp.bfloat16)
                plus = jnp.concatenate([plus[:, :TS], plus[:, TS:]], 0)
                fr = jnp.dot(inv_left_ref[:TS], plus, preferred_element_type=f32)
                minus = jnp.concatenate([ar - br, ai - bi], 1).astype(jnp.bfloat16)
                minus = jnp.dot(minus, inv_right_ref[...], preferred_element_type=f32).astype(jnp.bfloat16)
                minus = jnp.concatenate([minus[:, :TS], minus[:, TS:]], 0)
                fi = jnp.dot(inv_left_ref[TS:], minus, preferred_element_type=f32)
                band_at, column_at, there = tile_at(gy, gx)
                width = width_ref[band_at, column_at]
                pc = phasor_ref[0, band_at, column_at] * there
                ps = phasor_ref[1, band_at, column_at] * there
                inside = in_window(row, width) & in_window(lane, width)
                placed = (jnp.where(inside, fr * pc - fi * ps, 0.0), jnp.where(inside, fr * ps + fi * pc, 0.0))
                start = MARGIN + gx * INNER
                shift = start % TS
                rows = slice(gy * INNER, gy * INNER + TS)
                for part in range(2):
                    turned = pltpu.roll(placed[part], shift, 1)
                    canvas[start // TS, part, rows] += jnp.where(lane >= shift, turned, 0.0)
                    canvas[start // TS + 1, part, rows] += jnp.where(lane >= shift, 0.0, turned)
        left_out[...] = canvas[0].astype(left_out.dtype)
        mid_out[...] = canvas[1]
        right_out[...] = canvas[2].astype(right_out.dtype)


def deconvolve(plan, place, widths, phasors, weights, own, got, filt):
    chunk = plan.chunk
    y = np.arange(INNER)
    index = np.arange(TS)
    mid = as_bf16(forward_left(y + MARGIN))
    edge = np.stack([as_bf16(forward_left(y[:HALF] + TS - HALF)), as_bf16(forward_left(y[:HALF]))])
    wave = np.stack([np.cos(2 * math.pi * index / TS), np.sin(2 * math.pi * index / TS)])
    wave = np.broadcast_to(wave[:, :, None], (2, TS, TS)).astype(np.float32)
    shifts = np.arange(RW) - RW // 2
    theta = 2.0 * math.pi * (shifts[:, None] * index[None, :] % TS) / TS
    row = np.stack([np.cos(theta), np.sin(theta)]).astype(np.float32)
    inv_right, inv_left = inverse_tables()
    rows = (GY + 1) * INNER
    edge_canvas = jax.ShapeDtypeStruct((2, rows, TS), jnp.bfloat16)
    feed = pl.BlockSpec((chunk, INNER, TS), lambda i: (i, 0, 0))
    return pl.pallas_call(
        functools.partial(decon_kernel, plan),
        out_shape=(edge_canvas, jax.ShapeDtypeStruct((2, rows, TS), jnp.float32), edge_canvas),
        grid=(plan.steps,),
        in_specs=[
            smem(),
            smem(),
            smem(),
            smem(),
            smem(),
            feed,
            feed,
            pl.BlockSpec((chunk, 2, TS, TS), lambda i: (i, 0, 0, 0)),
            full(GX, 2, TS, 2 * TS),
            full(2 * TS, 2 * INNER),
            full(2, 2 * TS, 2 * HALF),
            full(2, TS, TS),
            full(2, RW, TS),
            full(2 * TS, 2 * TS),
            full(2 * TS, 2 * TS),
        ],
        out_specs=(full(2, rows, TS),) * 3,
        scratch_shapes=[
            pltpu.VMEM((GY, GX, 2 * TS, 2 * TS), jnp.bfloat16),
            pltpu.VMEM((2, GX, 2 * TS, 2 * HALF), jnp.bfloat16),
            pltpu.VMEM((GY, GX, 4, TS, TS), jnp.float32),
            pltpu.VMEM((GX, 2 * INNER, chunk * TS), jnp.bfloat16),
            pltpu.VMEM((2, GX, 2 * HALF, chunk * TS), jnp.bfloat16),
            pltpu.VMEM((GX, GY, 2 * TS, chunk * TS), jnp.float32),
            pltpu.VMEM((HIGHEST_RY, 2, TS, TS), jnp.float32),
            pltpu.VMEM((chunk, 4, TS, TS), jnp.float32),
            pltpu.VMEM((3, 2, rows, TS), jnp.float32),
        ],
        compiler_params=pltpu.CompilerParams(vmem_limit_bytes=58 * MIB),
        name="deconvolve",
    )(
        place,
        widths,
        phasors,
        jnp.asarray(plan.shift_tables()),
        weights,
        own,
        got,
        filt,
        jnp.asarray(plan.scan_tables()),
        jnp.asarray(mid),
        jnp.asarray(edge),
        jnp.asarray(wave),
        jnp.asarray(row),
        jnp.asarray(as_bf16(inv_right)),
        jnp.asarray(as_bf16(inv_left)),
    )


def passed_along(value, axis, steps):
    count = lax.axis_size(axis)
    leading, last = (max(0, -steps), min(count, count - steps))
    if leading >= last:
        return jnp.zeros_like(value)
    return lax.ppermute(value, axis, [(source, source + steps) for source in range(leading, last)])


def gathered(value, axis):
    count = lax.axis_size(axis)
    copies = jnp.broadcast_to(value[None], (count,) + value.shape)
    return lax.all_to_all(copies, axis, split_axis=0, concat_axis=0, tiled=True)


def own_rows(value):
    bands = lax.axis_size("band")
    sent = value.astype(jnp.bfloat16)
    first = MARGIN + INNER
    if bands > 4:
        mine = (
            value[:, first : first + INNER]
            + passed_along(sent[:, first + INNER : first + 2 * INNER], "band", 1)
            + passed_along(sent[:, MARGIN:first], "band", -1)
        )
        far_down = passed_along(sent[:, first + 2 * INNER :], "band", 2)
        far_up = passed_along(sent[:, :MARGIN], "band", -2)
        return mine + jnp.concatenate([far_down, far_up], 1)
    zero = jnp.zeros((), jnp.int32)
    band = lax.axis_index("band").astype(jnp.int32)
    scan = jnp.zeros((2, (bands + 4) * INNER, TS), jnp.bfloat16)
    scan = lax.dynamic_update_slice(scan, sent, (zero, band * INNER + 2 * INNER - first, zero))
    scan = scan[:, 2 * INNER : (bands + 2) * INNER].reshape(2, bands, INNER, TS)
    taken = lax.all_to_all(scan, "band", split_axis=1, concat_axis=1, tiled=True)
    return jnp.sum(taken.astype(jnp.float32), 1)


def own_part(plan, value, member):
    count = lax.axis_size("tile")
    if plan.group != 2:
        return lax.psum_scatter(
            value, "tile", scatter_dimension=2, axis_index_groups=plan.groups(count), tiled=True
        )
    zero = jnp.zeros((), jnp.int32)
    size = value.shape[:2] + (plan.cols,)
    kept = lax.dynamic_slice(value, (zero, zero, member * plan.cols), size)
    sent = lax.dynamic_slice(value, (zero, zero, (1 - member) * plan.cols), size)
    return kept + lax.ppermute(sent, "tile", [(i, i ^ 1) for i in range(count)])


def coverage(widths, inner, row_start, rows, col_start, cols):
    bands_n, per_band = widths.shape
    flat = jnp.arange(bands_n * per_band, dtype=jnp.int32)
    tile_band = flat // per_band
    tile_col = flat % per_band
    width = widths.reshape(-1)
    row_ids = row_start + jnp.arange(rows, dtype=jnp.int32)
    col_ids = col_start + jnp.arange(cols, dtype=jnp.int32)
    row_in = (
        (row_ids[None, :] >= (tile_band * inner - width)[:, None])
        & (row_ids[None, :] < (tile_band * inner + inner + width)[:, None])
    ).astype(jnp.float32)
    col_in = (
        (col_ids[None, :] >= (tile_col * inner - width)[:, None])
        & (col_ids[None, :] < (tile_col * inner + inner + width)[:, None])
    ).astype(jnp.float32)
    return jnp.dot(row_in.T, col_in, precision=lax.Precision.HIGHEST)


def local(frames, probe, rho_weights, phase_offsets, margin_widths):
    band = lax.axis_index("band").astype(jnp.int32)
    column = lax.axis_index("tile").astype(jnp.int32)
    plan = Plan(frames.shape[1], rho_weights.shape[1])
    member = column % plan.group
    side = member if plan.group == 2 else jnp.zeros((), jnp.int32)
    place = jnp.stack([band, column // plan.group, member, side])
    weights = gathered(rho_weights, "tile")
    angle = phase_offsets.astype(jnp.float32) * (2.0 * math.pi / phase_steps)
    phasors = jnp.stack([jnp.cos(angle), jnp.sin(angle)])
    own, got = shared_spectra(plan, place, frames)
    filt = filters(plan, place, probe)
    left, mid, right = deconvolve(plan, place, margin_widths, phasors, weights, own, got, filt)
    mid = mid + passed_along(left, "tile", -plan.group) + passed_along(right, "tile", plan.group)
    mine = own_rows(mid)
    total = own_part(plan, mine, member)
    count = coverage(margin_widths, INNER, band * INNER, INNER, column * plan.cols, plan.cols)
    return total / count[None]


def solution(mesh):
    return jax.shard_map(
        local,
        mesh=mesh,
        in_specs=(P("band", "tile", None), P(), P(None, "tile"), P(), P()),
        out_specs=P(None, "band", "tile"),
        check_vma=False,
    )
```

```python
import functools
import math

import jax
import jax.numpy as jnp
import numpy as np
from jax import lax
from jax.experimental import pallas as pl
from jax.experimental.pallas import tpu as pltpu
from jax.sharding import PartitionSpec as P

DY = 32
DX = 32
RW = 16
TS = 128
MARGIN = 32
INNER = TS - 2 * MARGIN
HALF = INNER // 2
GY = 3
GX = 4
phase_steps = 1024.0

MIB = 1024 * 1024


class Plan:
    def __init__(self, cols, held):
        lo = -(RW // 2)
        paired, alone = [], []
        for ry in range(lo, lo + RW):
            for rx in range(lo, lo + RW):
                if ry == lo or rx == lo or (ry == 0 and rx == 0):
                    alone.append((ry, rx))
                elif ry > 0 or (ry == 0 and rx > 0):
                    paired.append((ry, rx))
        self.cols = cols
        self.held = held
        self.group = TS // cols
        self.lists = [paired[c :: self.group] + alone[c :: self.group] for c in range(self.group)]
        self.paired = len(paired) // self.group
        self.share = len(self.lists[0])
        self.chunk = 8 if self.share % 8 == 0 else 2
        self.steps = self.share // self.chunk
        self.paired_steps = -(-self.paired // self.chunk)

    def shift_tables(self):
        rows = np.zeros((self.group, 6, self.share), np.int32)
        for c in range(self.group):
            for i, (ry, rx) in enumerate(self.lists[c]):
                rows[c, 0, i] = ry
                rows[c, 1, i] = rx
                partner = rho_of(-ry, -rx) if i < self.paired else rho_of(ry, rx)
                rows[c, 2:4, i] = divmod(rho_of(ry, rx), self.held)
                rows[c, 4:6, i] = divmod(partner, self.held)
        return rows

    def groups(self, count):
        return [list(range(at, at + self.group)) for at in range(0, count, self.group)]

    def scan_tables(self):
        x = np.arange(self.cols)
        halves = []
        for gx in range(GX):
            rows = [forward_right(c * self.cols + x - (gx - 1) * INNER + MARGIN) for c in range(self.group)]
            halves.append(np.concatenate(rows).reshape(2, TS, 2 * TS))
        return as_bf16(np.stack(halves))


HIGHEST_RY = RW // 2


def rho_of(ry, rx):
    return (ry + RW // 2) * RW + rx + RW // 2


def detector_table(order):
    ky = np.arange(DY)
    kx = np.arange(DX)
    out = np.zeros((2, len(order), DY * DX), np.float64)
    for i, (ry, rx) in enumerate(order):
        turns = ((ry * ky) % DY)[:, None] / DY + ((rx * kx) % DX)[None, :] / DX
        theta = 2.0 * math.pi * turns.reshape(-1)
        out[0, i] = np.cos(theta)
        out[1, i] = np.sin(theta)
    return as_bf16(out.reshape(2 * len(order), DY * DX) / math.sqrt(DY * DX))


def waves():
    index = np.arange(TS)
    theta = 2.0 * math.pi * (index[:, None] * index[None, :] % TS) / TS
    return np.cos(theta) / math.sqrt(TS), np.sin(theta) / math.sqrt(TS)


def forward_right(positions):
    cosine, sine = waves()
    valid = ((positions >= 0) & (positions < TS)).astype(np.float64)[:, None]
    at = np.clip(positions, 0, TS - 1)
    c, s = cosine[at] * valid, sine[at] * valid
    return np.block([[c, -s], [s, c]])


def forward_left(positions):
    return forward_right(positions).T


def inverse_tables():
    cosine, sine = waves()
    right = np.block([[cosine, sine], [-sine, cosine]]).astype(np.float32)
    real = np.concatenate([cosine, -sine], 1).astype(np.float32)
    imag = np.concatenate([sine, cosine], 1).astype(np.float32)
    return right, np.concatenate([real, imag], 0)


def as_bf16(table):
    return table.astype(np.float32).astype(jnp.bfloat16)


def iota(shape, dim):
    return lax.broadcasted_iota(jnp.int32, shape, dim)


ROWS_AT_ONCE = 16


def detector_kernel(table_ref, frames_ref, own_ref, other_ref, buf):
    share = own_ref.shape[0]
    both = 2 * share
    table = table_ref[0]
    lane = iota((both, TS), 1)
    low = lane < INNER
    for part in range(2):
        rows = ROWS_AT_ONCE // 2
        block = frames_ref[part * rows : (part + 1) * rows].reshape(rows * INNER, DY * DX)
        out = lax.dot_general(table, block, (((1,), (1,)), ((), ())), preferred_element_type=jnp.float32)
        for pair in range(rows // 2):
            c = out[:both, pair * TS : (pair + 1) * TS]
            s = out[both:, pair * TS : (pair + 1) * TS]
            first = jnp.where(low, c, pltpu.roll(s, INNER, 1))
            second = jnp.where(low, pltpu.roll(c, INNER, 1), s)
            y = part * rows + pair * 2
            buf[pl.ds(y, both, stride=ROWS_AT_ONCE), :] = first
            buf[pl.ds(y + 1, both, stride=ROWS_AT_ONCE), :] = second
    own_ref[...] = buf[: share * ROWS_AT_ONCE].reshape(share, ROWS_AT_ONCE, TS).astype(jnp.bfloat16)
    other_ref[...] = buf[share * ROWS_AT_ONCE :].reshape(share, ROWS_AT_ONCE, TS).astype(jnp.bfloat16)


def detector(plan, place, frames):
    share = plan.share
    tables = jnp.asarray(np.stack([detector_table(plan.lists[c] + plan.lists[1 - c]) for c in range(2)]))
    shape = jax.ShapeDtypeStruct((share, INNER, TS), jnp.bfloat16)
    spec = pl.BlockSpec((share, ROWS_AT_ONCE, TS), lambda i, place: (0, i, 0))

    def body(place_ref, *refs):
        detector_kernel(*refs)

    return pl.pallas_call(
        body,
        out_shape=(shape, shape),
        grid_spec=pltpu.PrefetchScalarGridSpec(
            num_scalar_prefetch=1,
            grid=(INNER // ROWS_AT_ONCE,),
            in_specs=[
                pl.BlockSpec((1, 4 * share, DY * DX), lambda i, place: (place[2], 0, 0)),
                pl.BlockSpec((ROWS_AT_ONCE, INNER, DY * DX), lambda i, place: (i, 0, 0)),
            ],
            out_specs=[spec, spec],
            scratch_shapes=[pltpu.VMEM((2 * share * ROWS_AT_ONCE, TS), jnp.float32)],
        ),
        compiler_params=pltpu.CompilerParams(vmem_limit_bytes=58 * MIB),
        name="detector",
    )(place, tables, frames)


def detector_any(plan, frames):
    rows, cols, pixels = frames.shape
    table = detector_table([rho for part in plan.lists for rho in part])
    spectra = lax.dot_general(
        jnp.asarray(table),
        frames.reshape(rows * cols, pixels),
        (((1,), (1,)), ((), ())),
        preferred_element_type=jnp.float32,
    ).astype(jnp.bfloat16)
    spectra = spectra.reshape(2, plan.group, plan.share, rows, cols)
    return jnp.transpose(spectra, (1, 2, 3, 0, 4)).reshape(plan.group, plan.share, rows, 2 * cols)


def shared_spectra(plan, place, frames):
    count = lax.axis_size("tile")
    if plan.group == 2:
        own, other = detector(plan, place, frames)
        return own, lax.ppermute(other, "tile", [(i, i ^ 1) for i in range(count)])
    spectra = detector_any(plan, frames)
    taken = lax.all_to_all(
        spectra, "tile", split_axis=0, concat_axis=0, axis_index_groups=plan.groups(count), tiled=True
    )
    taken = jnp.transpose(taken.reshape(2, plan.group // 2, plan.share, INNER, 2 * plan.cols), (0, 2, 3, 1, 4))
    taken = taken.reshape(2, plan.share, INNER, TS)
    return taken[0], taken[1]


ROW_BLOCK = 8


def filter_kernel(plan, place_ref, shift_ref, probe_ref, right_ref, left_ref, out_ref, first_buf, stack_buf, chi_buf):
    member = place_ref[2]
    step = pl.program_id(0)
    chunk = plan.chunk
    for pair in range(0, chunk, 2):
        lanes = slice(pair * TS, (pair + 2) * TS)
        for part in range(2):
            rows = slice(part * TS, (part + 1) * TS)
            chi_buf[rows, lanes] = jnp.dot(left_ref[rows], stack_buf[:, lanes], preferred_element_type=jnp.float32)
    for r in range(chunk):
        lanes = slice(r * TS, (r + 1) * TS)
        for start in range(0, TS, 2 * ROW_BLOCK):
            cr = chi_buf[start : start + 2 * ROW_BLOCK, lanes]
            ci = chi_buf[TS + start : TS + start + 2 * ROW_BLOCK, lanes]
            inv = 1.0 / (cr * cr + ci * ci + 1.0)
            out_ref[r, 0, start : start + 2 * ROW_BLOCK] = (cr * inv).astype(jnp.bfloat16)
            out_ref[r, 1, start : start + 2 * ROW_BLOCK] = (-ci * inv).astype(jnp.bfloat16)
    base_r, base_i = probe_ref[0], probe_ref[1]
    for r in range(chunk):
        at = jnp.minimum(step * chunk + r, plan.share - 1)
        back_y = lax.rem(TS - shift_ref[member, 0, at], TS)
        back_x = lax.rem(TS - shift_ref[member, 1, at], TS)
        moved_r = pltpu.roll(pltpu.roll(base_r, back_y, 0), back_x, 1)
        moved_i = pltpu.roll(pltpu.roll(base_i, back_y, 0), back_x, 1)
        real = base_r * moved_r + base_i * moved_i
        imag = base_i * moved_r - base_r * moved_i
        first_buf[r, :, :TS] = real.astype(jnp.bfloat16)
        first_buf[r, :, TS:] = imag.astype(jnp.bfloat16)
        middle = jnp.dot(first_buf[r], right_ref[...], preferred_element_type=jnp.float32).astype(jnp.bfloat16)
        for p in range(2):
            stack_buf[p * TS : (p + 1) * TS, r * TS : (r + 1) * TS] = middle[:, p * TS : (p + 1) * TS]


def smem():
    return pl.BlockSpec(memory_space=pltpu.SMEM)


def full(*shape):
    return pl.BlockSpec(shape, lambda i: (0,) * len(shape))


def filters(plan, place, probe):
    chunk = plan.chunk
    right = forward_right(np.arange(TS))
    return pl.pallas_call(
        functools.partial(filter_kernel, plan),
        out_shape=jax.ShapeDtypeStruct((plan.share, 2, TS, TS), jnp.bfloat16),
        grid=(plan.steps + 1,),
        in_specs=[smem(), smem(), full(2, TS, TS), full(2 * TS, 2 * TS), full(2 * TS, 2 * TS)],
        out_specs=pl.BlockSpec((chunk, 2, TS, TS), lambda i: (jnp.maximum(i - 1, 0), 0, 0, 0)),
        scratch_shapes=[
            pltpu.VMEM((chunk, TS, 2 * TS), jnp.bfloat16),
            pltpu.VMEM((2 * TS, chunk * TS), jnp.bfloat16),
            pltpu.VMEM((2 * TS, chunk * TS), jnp.float32),
        ],
        compiler_params=pltpu.CompilerParams(vmem_limit_bytes=58 * MIB),
        name="filters",
    )(place, jnp.asarray(plan.shift_tables()), probe, jnp.asarray(as_bf16(right)), jnp.asarray(as_bf16(right.T)))


def in_window(index, width):
    return (index >= MARGIN - width) & (index < TS - MARGIN + width)


def interleave(items, parts):
    done = 0
    for i, part in enumerate(parts):
        while done < len(items) and done * len(parts) <= i * len(items):
            items[done]()
            done += 1
        part()
    for item in items[done:]:
        item()


def decon_kernel(plan, place_ref, width_ref, phasor_ref, shift_ref, weight_ref, own_ref, got_ref, filt_ref,
                 cols_ref, mid_ref, edge_ref, wave_ref, row_ref, inv_right_ref, inv_left_ref,
                 left_out, mid_out, right_out,
                 cols_buf, edge_buf, acc, z_mid, z_edge, s_buf, ey, gains, canvas):
    step = pl.program_id(0)
    band = place_ref[0]
    chip = place_ref[1]
    member = place_ref[2]
    side_first = place_ref[3]
    chunk = plan.chunk
    f32 = jnp.float32

    def tile_at(gy, gx):
        bands, columns = width_ref.shape
        row = band + gy - 1
        column = 2 * chip + gx - 1
        real = (row >= 0) & (row < bands) & (column >= 0) & (column < columns)
        return jnp.clip(row, 0, bands - 1), jnp.clip(column, 0, columns - 1), real.astype(f32)

    def width_of(gy, gx):
        row, column, _ = tile_at(gy, gx)
        return width_ref[row, column]

    def prepare():
        row = iota((TS, 2 * TS), 0)
        x = row // (2 * plan.cols) * plan.cols + row % plan.cols
        lane = iota((2 * TS, 2 * HALF), 1)
        y = jnp.where(lane < HALF, lane, lane - HALF)
        for gx in range(GX):
            for o in range(2):
                side = side_first if o == 0 else 1 - side_first
                table = cols_ref[gx, pl.ds(side, 1)][0].astype(f32)
                xt = side * INNER + x - (gx - 1) * INNER + MARGIN
                for gy in range(GY):
                    width = width_of(gy, gx)
                    kept = jnp.where(in_window(xt, width), table, 0.0)
                    cols_buf[gy, gx, o * TS : (o + 1) * TS] = kept.astype(jnp.bfloat16)
            for e in range(2):
                width = width_of(2 * e, gx)
                yt = y + (TS - HALF if e == 0 else 0)
                kept = jnp.where(in_window(yt, width), edge_ref[e].astype(f32), 0.0)
                edge_buf[e, gx] = kept.astype(jnp.bfloat16)
        acc[...] = jnp.zeros(acc.shape, f32)
        ey[0, 0] = jnp.ones((TS, TS), f32)
        ey[0, 1] = jnp.zeros((TS, TS), f32)
        for n in range(1, HIGHEST_RY):
            r, i = ey[n - 1, 0], ey[n - 1, 1]
            a, b = wave_ref[0], wave_ref[1]
            ey[n, 0] = r * a - i * b
            ey[n, 1] = r * b + i * a

    def put(buf, at, z, rows):
        z = z.astype(jnp.bfloat16)
        for r in range(chunk):
            for p in range(2):
                buf[at + (slice(p * rows, (p + 1) * rows), slice(r * TS, (r + 1) * TS))] = z[
                    r * rows : (r + 1) * rows, p * TS : (p + 1) * TS
                ]

    def data(first, last):
        rows = last - first
        own = own_ref[:, first:last, :].reshape(chunk * rows, TS)
        got = got_ref[:, first:last, :].reshape(chunk * rows, TS)
        return jnp.concatenate([own, got], 1)

    def x_items(gx):
        def item(gy):
            first, last = ((0, HALF), (0, INNER), (HALF, INNER))[gy]
            z = jnp.dot(data(first, last), cols_buf[gy, gx], preferred_element_type=f32)
            if gy == 1:
                put(z_mid, (gx,), z, INNER)
            else:
                put(z_edge, (gy // 2, gx), z, HALF)

        return [functools.partial(item, gy) for gy in range(GY)]

    def y_items(gx):
        def item(gy, lanes, rows):
            if gy == 1:
                s = jnp.dot(mid_ref[rows], z_mid[gx, :, lanes], preferred_element_type=f32)
            else:
                s = jnp.dot(edge_buf[gy // 2, gx, rows], z_edge[gy // 2, gx, :, lanes], preferred_element_type=f32)
            s_buf[gx, gy, rows, lanes] = s

        return [
            functools.partial(item, gy, slice(at, at + 2 * TS), slice(part, part + TS))
            for gy in range(GY)
            for at in range(0, chunk * TS, 2 * TS)
            for part in (0, TS)
        ]

    def gain_parts(with_b):
        def part(r, at0):
            rows = slice(at0, at0 + 2 * ROW_BLOCK)
            at = step * chunk + r
            hr = filt_ref[r, 0, rows].astype(f32)
            hi = filt_ref[r, 1, rows].astype(f32)
            wr = weight_ref[shift_ref[member, 2, at], 0, shift_ref[member, 3, at]]
            wi = weight_ref[shift_ref[member, 2, at], 1, shift_ref[member, 3, at]]
            gains[r, 0, rows] = wr * hr - wi * hi
            gains[r, 1, rows] = wr * hi + wi * hr
            if with_b:
                keep = (at < plan.paired).astype(f32)
                vr = weight_ref[shift_ref[member, 4, at], 0, shift_ref[member, 5, at]] * keep
                vi = -weight_ref[shift_ref[member, 4, at], 1, shift_ref[member, 5, at]] * keep
                n = jnp.clip(shift_ref[member, 0, at], 0, HIGHEST_RY - 1)
                turn = shift_ref[member, 1, at] + RW // 2
                ex_r = row_ref[0, pl.ds(turn, 1), :]
                ex_i = row_ref[1, pl.ds(turn, 1), :]
                er = jnp.broadcast_to(vr * ex_r - vi * ex_i, (2 * ROW_BLOCK, TS))
                ei = jnp.broadcast_to(vr * ex_i + vi * ex_r, (2 * ROW_BLOCK, TS))
                yr = ey[n, 0, rows]
                yi = ey[n, 1, rows]
                pr = yr * er - yi * ei
                pi = yr * ei + yi * er
                gains[r, 2, rows] = pr * hr - pi * hi
                gains[r, 3, rows] = pr * hi + pi * hr

        starts = range(0, TS, 2 * ROW_BLOCK)
        return [functools.partial(part, r, at) for at in starts for r in range(chunk)]

    def gather_parts(gx, with_b):
        sums_n = 4 if with_b else 2

        def part(v):
            rows = slice(v * ROW_BLOCK, (v + 1) * ROW_BLOCK)
            low = slice(TS + v * ROW_BLOCK, TS + (v + 1) * ROW_BLOCK)
            sums = [[acc[gy, gx, c, rows] for c in range(sums_n)] for gy in range(GY)]
            for r in range(chunk):
                lanes = slice(r * TS, (r + 1) * TS)
                g = [gains[r, c, rows] for c in range(sums_n)]
                for gy in range(GY):
                    sr = s_buf[gx, gy, rows, lanes]
                    si = s_buf[gx, gy, low, lanes]
                    for c in range(0, sums_n, 2):
                        sums[gy][c] = sums[gy][c] + (g[c] * sr - g[c + 1] * si)
                        sums[gy][c + 1] = sums[gy][c + 1] + (g[c] * si + g[c + 1] * sr)
            for gy in range(GY):
                for c in range(sums_n):
                    acc[gy, gx, c, rows] = sums[gy][c]

        return [functools.partial(part, v) for v in range(TS // ROW_BLOCK)]

    def run(with_b):
        for part in gain_parts(with_b):
            part()
        for gx in range(GX):
            for item in x_items(gx):
                item()
        for item in y_items(0):
            item()
        for gx in range(GX):
            interleave(y_items(gx + 1) if gx + 1 < GX else [], gather_parts(gx, with_b))

    @pl.when(step == 0)
    def _():
        prepare()

    @pl.when(step < plan.paired_steps)
    def _():
        run(True)

    @pl.when(step >= plan.paired_steps)
    def _():
        run(False)

    @pl.when(step == plan.steps - 1)
    def _():
        canvas[...] = jnp.zeros(canvas.shape, f32)
        row = iota((TS, TS), 0)
        lane = iota((TS, TS), 1)
        for gy in range(GY):
            for gx in range(GX):
                ar, ai, br, bi = [acc[gy, gx, c] for c in range(4)]
                plus = jnp.concatenate([ar + br, ai + bi], 1).astype(jnp.bfloat16)
                plus = jnp.dot(plus, inv_right_ref[...], preferred_element_type=f32).astype(jnp.bfloat16)
                plus = jnp.concatenate([plus[:, :TS], plus[:, TS:]], 0)
                fr = jnp.dot(inv_left_ref[:TS], plus, preferred_element_type=f32)
                minus = jnp.concatenate([ar - br, ai - bi], 1).astype(jnp.bfloat16)
                minus = jnp.dot(minus, inv_right_ref[...], preferred_element_type=f32).astype(jnp.bfloat16)
                minus = jnp.concatenate([minus[:, :TS], minus[:, TS:]], 0)
                fi = jnp.dot(inv_left_ref[TS:], minus, preferred_element_type=f32)
                band_at, column_at, there = tile_at(gy, gx)
                width = width_ref[band_at, column_at]
                pc = phasor_ref[0, band_at, column_at] * there
                ps = phasor_ref[1, band_at, column_at] * there
                inside = in_window(row, width) & in_window(lane, width)
                placed = (jnp.where(inside, fr * pc - fi * ps, 0.0), jnp.where(inside, fr * ps + fi * pc, 0.0))
                start = MARGIN + gx * INNER
                shift = start % TS
                rows = slice(gy * INNER, gy * INNER + TS)
                for part in range(2):
                    turned = pltpu.roll(placed[part], shift, 1)
                    canvas[start // TS, part, rows] += jnp.where(lane >= shift, turned, 0.0)
                    canvas[start // TS + 1, part, rows] += jnp.where(lane >= shift, 0.0, turned)
        left_out[...] = canvas[0].astype(left_out.dtype)
        mid_out[...] = canvas[1]
        right_out[...] = canvas[2].astype(right_out.dtype)


def deconvolve(plan, place, widths, phasors, weights, own, got, filt):
    chunk = plan.chunk
    y = np.arange(INNER)
    index = np.arange(TS)
    mid = as_bf16(forward_left(y + MARGIN))
    edge = np.stack([as_bf16(forward_left(y[:HALF] + TS - HALF)), as_bf16(forward_left(y[:HALF]))])
    wave = np.stack([np.cos(2 * math.pi * index / TS), np.sin(2 * math.pi * index / TS)])
    wave = np.broadcast_to(wave[:, :, None], (2, TS, TS)).astype(np.float32)
    shifts = np.arange(RW) - RW // 2
    theta = 2.0 * math.pi * (shifts[:, None] * index[None, :] % TS) / TS
    row = np.stack([np.cos(theta), np.sin(theta)]).astype(np.float32)
    inv_right, inv_left = inverse_tables()
    rows = (GY + 1) * INNER
    edge_canvas = jax.ShapeDtypeStruct((2, rows, TS), jnp.bfloat16)
    feed = pl.BlockSpec((chunk, INNER, TS), lambda i: (i, 0, 0))
    return pl.pallas_call(
        functools.partial(decon_kernel, plan),
        out_shape=(edge_canvas, jax.ShapeDtypeStruct((2, rows, TS), jnp.float32), edge_canvas),
        grid=(plan.steps,),
        in_specs=[
            smem(),
            smem(),
            smem(),
            smem(),
            smem(),
            feed,
            feed,
            pl.BlockSpec((chunk, 2, TS, TS), lambda i: (i, 0, 0, 0)),
            full(GX, 2, TS, 2 * TS),
            full(2 * TS, 2 * INNER),
            full(2, 2 * TS, 2 * HALF),
            full(2, TS, TS),
            full(2, RW, TS),
            full(2 * TS, 2 * TS),
            full(2 * TS, 2 * TS),
        ],
        out_specs=(full(2, rows, TS),) * 3,
        scratch_shapes=[
            pltpu.VMEM((GY, GX, 2 * TS, 2 * TS), jnp.bfloat16),
            pltpu.VMEM((2, GX, 2 * TS, 2 * HALF), jnp.bfloat16),
            pltpu.VMEM((GY, GX, 4, TS, TS), jnp.float32),
            pltpu.VMEM((GX, 2 * INNER, chunk * TS), jnp.bfloat16),
            pltpu.VMEM((2, GX, 2 * HALF, chunk * TS), jnp.bfloat16),
            pltpu.VMEM((GX, GY, 2 * TS, chunk * TS), jnp.float32),
            pltpu.VMEM((HIGHEST_RY, 2, TS, TS), jnp.float32),
            pltpu.VMEM((chunk, 4, TS, TS), jnp.float32),
            pltpu.VMEM((3, 2, rows, TS), jnp.float32),
        ],
        compiler_params=pltpu.CompilerParams(vmem_limit_bytes=58 * MIB),
        name="deconvolve",
    )(
        place,
        widths,
        phasors,
        jnp.asarray(plan.shift_tables()),
        weights,
        own,
        got,
        filt,
        jnp.asarray(plan.scan_tables()),
        jnp.asarray(mid),
        jnp.asarray(edge),
        jnp.asarray(wave),
        jnp.asarray(row),
        jnp.asarray(as_bf16(inv_right)),
        jnp.asarray(as_bf16(inv_left)),
    )


def passed_along(value, axis, steps):
    count = lax.axis_size(axis)
    leading, last = (max(0, -steps), min(count, count - steps))
    if leading >= last:
        return jnp.zeros_like(value)
    return lax.ppermute(value, axis, [(source, source + steps) for source in range(leading, last)])


def gathered(value, axis):
    count = lax.axis_size(axis)
    copies = jnp.broadcast_to(value[None], (count,) + value.shape)
    return lax.all_to_all(copies, axis, split_axis=0, concat_axis=0, tiled=True)


def own_rows(value):
    bands = lax.axis_size("band")
    sent = value.astype(jnp.bfloat16)
    first = MARGIN + INNER
    if bands > 4:
        mine = (
            value[:, first : first + INNER]
            + passed_along(sent[:, first + INNER : first + 2 * INNER], "band", 1)
            + passed_along(sent[:, MARGIN:first], "band", -1)
        )
        far_down = passed_along(sent[:, first + 2 * INNER :], "band", 2)
        far_up = passed_along(sent[:, :MARGIN], "band", -2)
        return mine + jnp.concatenate([far_down, far_up], 1)
    zero = jnp.zeros((), jnp.int32)
    band = lax.axis_index("band").astype(jnp.int32)
    scan = jnp.zeros((2, (bands + 4) * INNER, TS), jnp.bfloat16)
    scan = lax.dynamic_update_slice(scan, sent, (zero, band * INNER + 2 * INNER - first, zero))
    scan = scan[:, 2 * INNER : (bands + 2) * INNER].reshape(2, bands, INNER, TS)
    taken = lax.all_to_all(scan, "band", split_axis=1, concat_axis=1, tiled=True)
    return jnp.sum(taken.astype(jnp.float32), 1)


def own_part(plan, value, member):
    count = lax.axis_size("tile")
    if plan.group != 2:
        return lax.psum_scatter(
            value, "tile", scatter_dimension=2, axis_index_groups=plan.groups(count), tiled=True
        )
    zero = jnp.zeros((), jnp.int32)
    size = value.shape[:2] + (plan.cols,)
    kept = lax.dynamic_slice(value, (zero, zero, member * plan.cols), size)
    sent = lax.dynamic_slice(value, (zero, zero, (1 - member) * plan.cols), size)
    return kept + lax.ppermute(sent, "tile", [(i, i ^ 1) for i in range(count)])


def coverage(widths, inner, row_start, rows, col_start, cols):
    bands_n, per_band = widths.shape
    flat = jnp.arange(bands_n * per_band, dtype=jnp.int32)
    tile_band = flat // per_band
    tile_col = flat % per_band
    width = widths.reshape(-1)
    row_ids = row_start + jnp.arange(rows, dtype=jnp.int32)
    col_ids = col_start + jnp.arange(cols, dtype=jnp.int32)
    row_in = (
        (row_ids[None, :] >= (tile_band * inner - width)[:, None])
        & (row_ids[None, :] < (tile_band * inner + inner + width)[:, None])
    ).astype(jnp.float32)
    col_in = (
        (col_ids[None, :] >= (tile_col * inner - width)[:, None])
        & (col_ids[None, :] < (tile_col * inner + inner + width)[:, None])
    ).astype(jnp.float32)
    return jnp.dot(row_in.T, col_in, precision=lax.Precision.HIGHEST)


def local(frames, probe, rho_weights, phase_offsets, margin_widths):
    band = lax.axis_index("band").astype(jnp.int32)
    column = lax.axis_index("tile").astype(jnp.int32)
    plan = Plan(frames.shape[1], rho_weights.shape[1])
    member = column % plan.group
    side = member if plan.group == 2 else jnp.zeros((), jnp.int32)
    place = jnp.stack([band, column // plan.group, member, side])
    weights = gathered(rho_weights, "tile")
    angle = phase_offsets.astype(jnp.float32) * (2.0 * math.pi / phase_steps)
    phasors = jnp.stack([jnp.cos(angle), jnp.sin(angle)])
    own, got = shared_spectra(plan, place, frames)
    filt = filters(plan, place, probe)
    left, mid, right = deconvolve(plan, place, margin_widths, phasors, weights, own, got, filt)
    mid = mid + passed_along(left, "tile", -plan.group) + passed_along(right, "tile", plan.group)
    mine = own_rows(mid)
    total = own_part(plan, mine, member)
    count = coverage(margin_widths, INNER, band * INNER, INNER, column * plan.cols, plan.cols)
    return total / count[None]


def solution(mesh):
    return jax.shard_map(
        local,
        mesh=mesh,
        in_specs=(P("band", "tile", None), P(), P(None, "tile"), P(), P()),
        out_specs=P(None, "band", "tile"),
        check_vma=False,
    )
```
